32 devices in a mesh: tile: 8 (over z, y), hidden: 4 (over x, core).
Axes of the slice: x: 2, y: 2, z: 4, core: 2. Of those that a mesh axis runs over, the one named last changes fastest.
Arguments:
- cells: bfloat16 [128, 48, 48, 128], P(('tile', 'hidden')), may hold values from -6 to 6
- partner_edge: int32 [128, 4], P(('tile', 'hidden')), may hold values from 0 to 511, as said below
- edge_flip: int32 [128, 4], P(('tile', 'hidden')), may hold values from 0 to 1, as said below
- dw_weight: float32 [9, 128], replicated, may hold values from -2 to 2
- dw_bias: float32 [128], replicated, may hold values from -3 to 3
- ln_gain: float32 [128], replicated, may hold values from 0.5 to 1.5
- ln_bias: float32 [128], replicated, may hold values from -3 to 3
- w_in: bfloat16 [512, 128], replicated, may hold values from -0.5 to 0.5
- b_in: bfloat16 [512], replicated, may hold values from -3 to 3
- w_out: bfloat16 [512, 128], replicated, may hold values from -0.25 to 0.25
- b_out: float32 [128], replicated, may hold values from -3 to 3
- layer_scale: float32 [128], replicated, may hold values from 0.5 to 1.5
Outputs:
- updated: bfloat16 [128, 48, 48, 128], P(('tile', 'hidden'))
The draws below stay inside these ranges and needn't reach their ends.
Inputs may be any that keep to these rules, and one draw needn't show every extreme that they name: `partner_edge`: edges are matched in pairs: if edge a names edge b, then b names a, a != b, and both carry the same edge_flip. Every edge's partner lies on the same device as its tile or on the device just before or just after it in the order of tile+hidden, the last and the first being neighbours; exactly 4 edges of each device have partners on the next device. `edge_flip`: equal at the two edges of a matched pair.
All inputs are finite; a program needn't handle non-finite values.
Results may differ from the reference program's by a relative error of at most 0.0044.
Values may be sent and summed in bfloat16 or wider, within the bound.
A program may use at most 64 MiB of HBM per device.

```python
import jax
import jax.numpy as jnp
from jax import lax

C = 128
FFN = 512
TS = 48
TPD = 4
TILES = 128


def matching(key):
    base_key = jax.random.fold_in(key, 7)
    groups = TILES // TPD
    edge_count = 4 * TPD
    device_keys = jax.random.split(base_key, groups)
    orders = jax.vmap(lambda one_key: jax.random.permutation(one_key, edge_count))(device_keys)
    offsets = (jnp.arange(groups, dtype=jnp.int32) * edge_count)[:, None]
    going_right = orders[:, :TPD] + offsets
    going_left = orders[:, TPD:2 * TPD] + offsets
    left_next = jnp.roll(going_left, -1, axis=0)
    inner_edges = orders[:, 2 * TPD:] + offsets
    first_inner = inner_edges[:, 0::2]
    second_inner = inner_edges[:, 1::2]
    sources = jnp.concatenate([going_right.ravel(), left_next.ravel(), first_inner.ravel(), second_inner.ravel()])
    targets = jnp.concatenate([left_next.ravel(), going_right.ravel(), second_inner.ravel(), first_inner.ravel()])
    flip_key = jax.random.fold_in(base_key, 11)
    cross_flip = jax.random.randint(jax.random.fold_in(flip_key, 1), (groups * TPD,), 0, 2, dtype=jnp.int32)
    inner_flip = jax.random.randint(jax.random.fold_in(flip_key, 2), (groups * TPD,), 0, 2, dtype=jnp.int32)
    flip_values = jnp.concatenate([cross_flip, cross_flip, inner_flip, inner_flip])
    partner = jnp.zeros((groups * edge_count,), jnp.int32).at[sources].set(targets.astype(jnp.int32))
    flipped = jnp.zeros((groups * edge_count,), jnp.int32).at[sources].set(flip_values)
    return (partner.reshape(TILES, 4), flipped.reshape(TILES, 4))


def draw_partner_edge(key, part):
    return matching(key)[0]


def draw_edge_flip(key, part):
    return matching(key)[1]


def block_scale(stream_key, dims, pieces, least, largest):
    level, own = 1.0, jax.random.fold_in(stream_key, 6)
    for dim, shards_of in pieces:
        draws = jnp.exp(jax.random.uniform(jax.random.fold_in(own, dim), (shards_of,), jnp.float32, least / len(pieces), largest / len(pieces)))
        level = level * jnp.repeat(draws, dims[dim] // shards_of).reshape([-1 if axis == dim else 1 for axis in range(len(dims))])
    return level


def gaussian(own_key, extent, width, limit, cuts=(), kind=jnp.bfloat16):
    level = block_scale(own_key, extent, cuts, -0.22, 0.18) if cuts else 1.0
    entries = jax.random.normal(own_key, extent, jnp.float32) * width * level
    return jnp.minimum(jnp.maximum(entries, -limit), limit).astype(kind)


def setup_inputs(seed: int = 0) -> dict:
    key_list = jax.random.split(jax.random.key(seed), 13)
    return {
        "cells": gaussian(key_list[0], (TILES, TS, TS, C), 1.0, 6.0, ((0, 32),)),
        "partner_edge": draw_partner_edge(jax.random.fold_in(key_list[12], 71), 0),
        "edge_flip": draw_edge_flip(jax.random.fold_in(key_list[12], 71), 0),
        "dw_weight": gaussian(key_list[3], (9, C), 9 ** -0.5, 2.0, (), jnp.float32),
        "dw_bias": gaussian(key_list[4], (C,), 0.5, 3.0, (), jnp.float32),
        "ln_gain": jnp.clip(1.0 + 0.1 * jax.random.normal(key_list[5], (C,), jnp.float32), 0.5, 1.5),
        "ln_bias": gaussian(key_list[6], (C,), 0.5, 3.0, (), jnp.float32),
        "w_in": gaussian(key_list[7], (FFN, C), C ** -0.5, 0.5),
        "b_in": gaussian(key_list[8], (FFN,), 0.5, 3.0),
        "w_out": gaussian(key_list[9], (FFN, C), FFN ** -0.5, 0.25),
        "b_out": gaussian(key_list[10], (C,), 0.5, 3.0, (), jnp.float32),
        "layer_scale": jnp.clip(jax.random.uniform(key_list[11], (C,), jnp.float32, 0.5, 1.5), 0.5, 1.5),
    }


def boundary(tiles_in):
    return jnp.stack([tiles_in[:, 0], tiles_in[:, :, -1], tiles_in[:, -1], tiles_in[:, :, 0]], axis=1)

def pad_tiles(tiles_in, halo_rows):
    north_rim = halo_rows[:, 0].astype(jnp.float32)
    east_rim = halo_rows[:, 1].astype(jnp.float32)
    south_rim = halo_rows[:, 2].astype(jnp.float32)
    west_rim = halo_rows[:, 3].astype(jnp.float32)
    top_row = jnp.concatenate([0.5 * (north_rim[:, :1] + west_rim[:, :1]), north_rim, 0.5 * (north_rim[:, -1:] + east_rim[:, :1])], axis=1)
    bottom_row = jnp.concatenate([0.5 * (south_rim[:, :1] + west_rim[:, -1:]), south_rim, 0.5 * (south_rim[:, -1:] + east_rim[:, -1:])], axis=1)
    middle = jnp.concatenate([west_rim[:, :, None], tiles_in.astype(jnp.float32), east_rim[:, :, None]], axis=2)
    return jnp.concatenate([top_row[:, None], middle, bottom_row[:, None]], axis=1)

def depthwise(padded, dw_weight, dw_bias):
    side_len = padded.shape[1] - 2
    total = jnp.zeros(padded[:, 1:-1, 1:-1].shape, jnp.float32) + dw_bias
    for row_tap in range(3):
        for col_tap in range(3):
            total = total + dw_weight[3 * row_tap + col_tap] * padded[:, row_tap:row_tap + side_len, col_tap:col_tap + side_len]
    return total

def layer_norm(conv, ln_gain, ln_bias):
    center = lax.optimization_barrier(jnp.mean(conv, axis=-1, keepdims=True))
    spread = lax.optimization_barrier(jnp.mean((conv - center) ** 2, axis=-1, keepdims=True))
    return ((conv - center) * lax.rsqrt(spread + 1e-06) * ln_gain + ln_bias).astype(jnp.bfloat16)

def reference(cells, partner_edge, edge_flip, dw_weight, dw_bias, ln_gain, ln_bias, w_in, b_in, w_out, b_out, layer_scale):
    tile_count, tile_side, _, channels = cells.shape
    edge_count = 4 * tile_count
    rims = boundary(cells).reshape(edge_count, tile_side, channels)
    halo_rows = rims[partner_edge.reshape(edge_count)]
    halo_rows = jnp.where(edge_flip.reshape(edge_count)[:, None, None] == 1, halo_rows[:, ::-1], halo_rows)
    halo_rows = halo_rows.reshape(tile_count, 4, tile_side, channels)

    def one_tile(pair):
        tile_in, tile_halo = pair
        padded = pad_tiles(tile_in[None], tile_halo[None])
        conv = depthwise(padded, dw_weight, dw_bias)
        normed = layer_norm(conv, ln_gain, ln_bias).reshape(-1, channels)
        pre = lax.dot_general(normed, w_in, (((1,), (1,)), ((), ())), preferred_element_type=jnp.float32) + b_in.astype(jnp.float32)
        act = jax.nn.gelu(pre, approximate=False).astype(jnp.bfloat16)
        mixed = jnp.dot(act, w_out, preferred_element_type=jnp.float32) + b_out
        mixed = mixed.reshape(tile_side, tile_side, channels)
        return (tile_in.astype(jnp.float32) + layer_scale * mixed).astype(jnp.bfloat16)
    return lax.map(one_tile, (cells, halo_rows))
```

```python
import functools

import jax
import jax.numpy as jnp
from jax import lax
from jax.experimental import pallas as pl
from jax.experimental.pallas import tpu as pltpu
from jax.sharding import PartitionSpec as P

AXES = ("tile", "hidden")
OFF = 8
ROWS = 8
UNROLL = 2
CROSS = 4
GRANT = 40 * 1024 * 1024
MESH = pl.DeviceIdType.MESH
ROOT_HALF = 0.7071067811865476


def tile_of(q, per_tile, tiles):
    tile = 0
    for j in range(1, tiles):
        tile = tile + jnp.where(q >= j * per_tile, 1, 0)
    return tile


def row_lines(pad_ref, side, tile, row):
    line = tile * (side + 2) + row
    return lambda a, b: pad_ref[line + a, pl.ds(OFF - 1 + b, side), :]


def col_lines(flat_pad, side, width, tile, col):
    first = tile * (side + 2) * width + OFF - 1 + col
    return lambda a, b: flat_pad[pl.ds(first + a * width + b, side, stride=width), :]


def conv(dw_ref, dw_bias_ref, side, segments, dst):
    channels = dw_ref.shape[1]
    for n, load in enumerate(segments):
        total = jnp.broadcast_to(dw_bias_ref[...], (side, channels))
        for a in range(3):
            for b in range(3):
                total = total + dw_ref[3 * a + b : 3 * a + b + 1] * load(a, b)
        center = total - jnp.mean(total, axis=-1, keepdims=True)
        spread = jnp.sum(center * center, axis=-1, keepdims=True)
        value = center * lax.rsqrt(spread + 1e-06 * channels)
        dst[n * side : (n + 1) * side, 0:channels] = value.astype(jnp.bfloat16)


def mlp(w_aug_ref, w_fin_ref, bias_ref, side, segments, src):
    z = jnp.dot(src[...], w_aug_ref[...], preferred_element_type=jnp.float32)
    z = z.astype(jnp.bfloat16)
    act = z * (lax.erf(z) + jnp.bfloat16(1))
    mixed = jnp.dot(act, w_fin_ref[...], preferred_element_type=jnp.float32)
    for n, (load, store) in enumerate(segments):
        store(load(1, 1) + (mixed[n * side : (n + 1) * side] + bias_ref[...]))


def fill_ones(buf):
    rows, both = buf.shape
    lane = lax.broadcasted_iota(jnp.int32, (rows, both // 2), 1)
    buf[:, both // 2 :] = jnp.where(lane < 2, 1.0, 0.0).astype(jnp.bfloat16)


def last_flagged(flags, values):
    found = [jnp.int32(0)] * CROSS
    for flag, value in zip(flags, values):
        for k in range(CROSS - 1, 0, -1):
            found[k] = jnp.where(flag, found[k - 1], found[k])
        found[0] = jnp.where(flag, value, found[0])
    return found


def owned(partner, device, edges):
    local = partner - device * edges
    return (local >= 0) & (local < edges), local


def above(values, limit):
    return sum(jnp.where(value > limit, 1, 0) for value in values)


def split_bf16(value):
    high = value.astype(jnp.bfloat16).astype(jnp.float32)
    return high, value - high


def fold_weights(gain_ref, ln_bias_ref, w_in, b_in, w_out, b_out_ref, scale_ref, w_aug_ref, w_fin_ref, bias_ref):
    hidden, channels = w_in.shape
    eye = (
        lax.broadcasted_iota(jnp.int32, (channels, channels), 0)
        == lax.broadcasted_iota(jnp.int32, (channels, channels), 1)
    ).astype(jnp.bfloat16)
    gain = gain_ref[...] * (ROOT_HALF * channels**0.5)
    w_gain = (w_in.astype(jnp.float32) * gain).astype(jnp.bfloat16)
    turned = (((1,), (1,)), ((), ()))
    w_aug_ref[0:channels, :] = lax.dot_general(
        eye, w_gain, turned, preferred_element_type=jnp.float32
    ).astype(jnp.bfloat16)
    high, rest = split_bf16(ln_bias_ref[...])
    middle, low = split_bf16(rest)
    row_id = lax.broadcasted_iota(jnp.int32, (16, channels), 0)
    parts = jnp.where(
        row_id == 0, high, jnp.where(row_id == 1, middle, jnp.where(row_id == 2, low, 0.0))
    ).astype(jnp.bfloat16)
    moved = lax.dot_general(parts, w_in, turned, preferred_element_type=jnp.float32)
    moved = jnp.sum(moved, axis=0, keepdims=True)
    total = (b_in.astype(jnp.float32).reshape(1, hidden) + moved) * ROOT_HALF
    high, rest = split_bf16(total)
    row_id = lax.broadcasted_iota(jnp.int32, (channels, hidden), 0)
    extra = jnp.where(row_id == 0, high, jnp.where(row_id == 1, rest, 0.0))
    w_aug_ref[channels : 2 * channels, :] = extra.astype(jnp.bfloat16)
    scale = scale_ref[...]
    w_fin_ref[...] = (w_out.astype(jnp.float32) * (scale * ROOT_HALF)).astype(jnp.bfloat16)
    bias_ref[...] = scale * b_out_ref[...]


def inner_kernel(
    sizes,
    cells_ref,
    partner_hbm,
    flip_hbm,
    dw_hbm,
    dw_bias_hbm,
    gain_hbm,
    ln_bias_hbm,
    w_in_hbm,
    b_in_hbm,
    w_out_hbm,
    b_out_hbm,
    scale_hbm,
    mid_ref,
    strip_ref,
    pad_ref,
    w_aug_ref,
    w_fin_ref,
    dw_ref,
    dw_bias_ref,
    bias_ref,
    cells_buf,
    rims_ref,
    recv_ref,
    send_buf,
    buf_a,
    buf_b,
    partner_ref,
    flip_ref,
    gain_ref,
    ln_bias_ref,
    w_in_ref,
    b_in_ref,
    w_out_ref,
    b_out_ref,
    scale_ref,
    load_sem,
    table_sem,
    weight_sem,
    send_sem,
    recv_sem,
):
    tile_devices, hidden_devices = sizes
    tiles, side, _, channels = cells_buf.shape
    edges = 4 * tiles
    width = side + 2 * OFF
    devices = tile_devices * hidden_devices
    me = lax.axis_index("tile") * hidden_devices + lax.axis_index("hidden")

    def at(position):
        return (position // hidden_devices, position % hidden_devices)

    right = lax.rem(me + 1, devices)
    left = lax.rem(me + devices - 1, devices)
    loads = [
        pltpu.make_async_copy(cells_ref.at[t], cells_buf.at[t], load_sem.at[t])
        for t in range(tiles)
    ]
    tables = [
        pltpu.make_async_copy(src, dst, table_sem.at[n])
        for n, (src, dst) in enumerate(((partner_hbm, partner_ref), (flip_hbm, flip_ref)))
    ]
    weights = [
        pltpu.make_async_copy(src, dst, weight_sem.at[n])
        for n, (src, dst) in enumerate(
            (
                (w_in_hbm, w_in_ref),
                (w_out_hbm, w_out_ref),
                (b_in_hbm, b_in_ref),
                (gain_hbm, gain_ref),
                (ln_bias_hbm, ln_bias_ref),
                (b_out_hbm, b_out_ref),
                (scale_hbm, scale_ref),
                (dw_hbm, dw_ref),
                (dw_bias_hbm, dw_bias_ref),
            )
        )
    ]
    for copy in tables + weights[:3] + loads[:1] + weights[3:] + loads[1:]:
        copy.start()
    barrier = pltpu.get_barrier_semaphore()
    for neighbour in (left, right):
        pl.semaphore_signal(barrier, inc=1, device_id=at(neighbour), device_id_type=MESH)

    fill_ones(buf_a)
    fill_ones(buf_b)
    for copy in weights:
        copy.wait()
    fold_weights(
        gain_ref,
        ln_bias_ref,
        w_in_ref[...],
        b_in_ref[...],
        w_out_ref[...],
        b_out_ref,
        scale_ref,
        w_aug_ref,
        w_fin_ref,
        bias_ref,
    )
    for copy in tables:
        copy.wait()
    partners = [partner_ref[e // 4, e % 4] for e in range(edges)]
    local = [jnp.int32(e) for e in range(edges)]
    going = []
    for device in (right, left):
        going += last_flagged([owned(p, device, edges)[0] for p in partners], local)

    flat_pad = pad_ref.reshape(tiles * (side + 2) * width, channels)
    for t in range(tiles):
        loads[t].wait()
        top = t * (side + 2)
        pad_ref[pl.ds(top + 1, side), pl.ds(OFF, side), :] = cells_buf[t].astype(jnp.float32)
        first = (top + 1) * width + OFF
        mine = 4 * t
        rims_ref[mine] = cells_buf[t, 0]
        rims_ref[mine + 2] = cells_buf[t, side - 1]
        east = flat_pad[pl.ds(first + side - 1, side, stride=width), :]
        rims_ref[mine + 1] = east.astype(jnp.bfloat16)
        west = flat_pad[pl.ds(first, side, stride=width), :]
        rims_ref[mine + 3] = west.astype(jnp.bfloat16)
    for k in range(2 * CROSS):
        send_buf[k] = rims_ref[going[k]]

    sends = [
        pltpu.make_async_remote_copy(
            src_ref=send_buf.at[pl.ds(side_id * CROSS, CROSS)],
            dst_ref=recv_ref.at[pl.ds(side_id * CROSS, CROSS)],
            send_sem=send_sem.at[side_id],
            recv_sem=recv_sem.at[side_id],
            device_id=at(target),
            device_id_type=MESH,
        )
        for side_id, target in ((0, right), (1, left))
    ]

    def send():
        pl.semaphore_wait(barrier, 2)
        for copy in sends:
            copy.start()

    inner_rows = side - 2

    def rows_of(chunk):
        found = []
        for k in range(ROWS):
            q = chunk * ROWS + k
            tile = tile_of(q, inner_rows, tiles)
            found.append((tile, q - inner_rows * tile + 1))
        return found

    def do_conv(chunk, dst):
        lines = [row_lines(pad_ref, side, tile, row) for tile, row in rows_of(chunk)]
        conv(dw_ref, dw_bias_ref, side, lines, dst)

    def put(tile, row):
        def store(new):
            mid_ref[tile, row] = new[OFF : side - OFF].astype(jnp.bfloat16)
            strip_ref[tile, row, 0:OFF, :] = new[:OFF]
            strip_ref[tile, row, OFF:, :] = new[side - OFF :]

        return store

    def do_mlp(chunk, src):
        lines = [
            (row_lines(pad_ref, side, tile, row), put(tile, row)) for tile, row in rows_of(chunk)
        ]
        mlp(w_aug_ref, w_fin_ref, bias_ref, side, lines, src)

    chunks = tiles * inner_rows // ROWS
    bufs = (buf_a, buf_b)
    do_conv(0, buf_a)
    rounds = (chunks - 1) // UNROLL
    turn = jnp.where(me == 0, rounds - 1, jnp.where(me == devices - 1, 0, min(2, rounds - 1)))

    @pl.loop(0, rounds)
    def _(i):
        @pl.when(i == turn)
        def _():
            send()

        for u in range(UNROLL):
            do_mlp(UNROLL * i + u, bufs[u % 2])
            do_conv(UNROLL * i + u + 1, bufs[(u + 1) % 2])

    for c in range((chunks - 1) // UNROLL * UNROLL, chunks):
        do_mlp(c, bufs[c % 2])
        if c + 1 < chunks:
            do_conv(c + 1, bufs[(c + 1) % 2])
    for copy in sends:
        copy.wait()

    prev_flags, prev_local = zip(*[owned(p, left, edges) for p in partners])
    next_flags, next_local = zip(*[owned(p, right, edges) for p in partners])
    prev_list = last_flagged(prev_flags, prev_local)
    next_list = last_flagged(next_flags, next_local)
    r_id = lax.broadcasted_iota(jnp.int32, (side, side), 0)
    c_id = lax.broadcasted_iota(jnp.int32, (side, side), 1)
    for t in range(tiles):
        lines = []
        for s in range(4):
            e = 4 * t + s
            is_prev, is_next = prev_flags[e], next_flags[e]
            slot = jnp.where(
                is_prev,
                above(prev_list, prev_local[e]),
                CROSS + above(next_list, next_local[e]),
            )
            crosses = is_prev | is_next
            own_edge = jnp.clip(jnp.where(crosses, 0, partners[e] - me * edges), 0, edges - 1)
            received = recv_ref[jnp.clip(jnp.where(crosses, slot, 0), 0, 2 * CROSS - 1)]
            line = jnp.where(crosses, received, rims_ref[own_edge])
            target = jnp.where(flip_ref[t, s] == 1, side - 1 - r_id, r_id)
            order = jnp.where(c_id == target, 1.0, 0.0).astype(jnp.bfloat16)
            lines.append(jnp.dot(order, line, preferred_element_type=jnp.float32))
        north, east, south, west = lines
        top = t * (side + 2)
        end = top + side + 1
        pad_ref[top, pl.ds(OFF, side), :] = north
        pad_ref[end, pl.ds(OFF, side), :] = south
        first = (top + 1) * width + OFF
        flat_pad[pl.ds(first - 1, side, stride=width), :] = west
        flat_pad[pl.ds(first + side, side, stride=width), :] = east
        pad_ref[top, OFF - 1 : OFF, :] = 0.5 * (north[:1] + west[:1])
        pad_ref[top, OFF + side : OFF + side + 1, :] = 0.5 * (north[-1:] + east[:1])
        pad_ref[end, OFF - 1 : OFF, :] = 0.5 * (south[:1] + west[-1:])
        pad_ref[end, OFF + side : OFF + side + 1, :] = 0.5 * (south[-1:] + east[-1:])


def edge_kernel(
    mid_ref,
    strip_in_ref,
    pad_ref,
    w_aug_ref,
    w_fin_ref,
    dw_ref,
    dw_bias_ref,
    bias_ref,
    out_hbm,
    strip_ref,
    caps_ref,
    sides_ref,
    buf_a,
    buf_b,
    mid_sem,
    cap_sem,
    side_sem,
):
    tiles, side, _, channels = out_hbm.shape
    width = side + 2 * OFF
    mid_copies = [
        pltpu.make_async_copy(
            mid_ref.at[t, pl.ds(1, side - 2)],
            out_hbm.at[t, pl.ds(1, side - 2), pl.ds(OFF, side - 2 * OFF)],
            mid_sem.at[t],
        )
        for t in range(tiles)
    ]
    for copy in mid_copies:
        copy.start()
    fill_ones(buf_a)
    fill_ones(buf_b)
    flat_pad = pad_ref.reshape(tiles * (side + 2) * width, channels)
    flat_strip = strip_ref.reshape(tiles * side * 2 * OFF, channels)

    def put_cap(tile, n):
        def store(new):
            caps_ref[tile, n] = new.astype(jnp.bfloat16)

        return store

    def put_side(tile, n):
        first = tile * side * 2 * OFF + n * (2 * OFF - 1)

        def store(new):
            flat_strip[pl.ds(first, side, stride=2 * OFF), :] = new

        return store

    def lines_of(tile):
        return [
            (row_lines(pad_ref, side, tile, 0), put_cap(tile, 0)),
            (row_lines(pad_ref, side, tile, side - 1), put_cap(tile, 1)),
            (col_lines(flat_pad, side, width, tile, 0), put_side(tile, 0)),
            (col_lines(flat_pad, side, width, tile, side - 1), put_side(tile, 1)),
        ]

    groups = [
        [line for t in range(g, g + 2) for line in lines_of(t)] for g in range(0, tiles, 2)
    ]
    bufs = (buf_a, buf_b)
    copies = []

    def finish(g):
        for t in (2 * g, 2 * g + 1):
            for n, row in enumerate((0, side - 1)):
                copies.append(
                    pltpu.make_async_copy(
                        caps_ref.at[t, n], out_hbm.at[t, row], cap_sem.at[t, n]
                    )
                )
                copies[-1].start()
            for n, col in enumerate((0, side - OFF)):
                sides_ref[t, n] = strip_ref[t, :, n * OFF : (n + 1) * OFF, :].astype(jnp.bfloat16)
                copies.append(
                    pltpu.make_async_copy(
                        sides_ref.at[t, n, pl.ds(1, side - 2)],
                        out_hbm.at[t, pl.ds(1, side - 2), pl.ds(col, OFF)],
                        side_sem.at[t, n],
                    )
                )
                copies[-1].start()

    for g, group in enumerate(groups):
        conv(dw_ref, dw_bias_ref, side, [load for load, _ in group], bufs[g % 2])
        if g:
            mlp(w_aug_ref, w_fin_ref, bias_ref, side, groups[g - 1], bufs[(g - 1) % 2])
            finish(g - 1)
    mlp(w_aug_ref, w_fin_ref, bias_ref, side, groups[-1], bufs[(len(groups) - 1) % 2])
    finish(len(groups) - 1)
    for copy in mid_copies + copies:
        copy.wait()


def per_device(sizes, cells, *rest):
    tables, (dw_weight, dw_bias, ln_gain, ln_bias, w_in, b_in, w_out, b_out, layer_scale) = (
        rest[:2],
        rest[2:],
    )
    tiles, side, _, channels = cells.shape
    hidden = w_in.shape[0]
    edges = 4 * tiles
    vmem = pl.BlockSpec(memory_space=pltpu.VMEM)
    anywhere = pl.BlockSpec(memory_space=pltpu.HBM)
    dw_bias, ln_gain, ln_bias, b_out, layer_scale = (
        vector.reshape(1, channels)
        for vector in (dw_bias, ln_gain, ln_bias, b_out, layer_scale)
    )
    operands = [
        pltpu.with_memory_space_constraint(array, pltpu.HBM)
        for array in (
            cells,
            *tables,
            dw_weight,
            dw_bias,
            ln_gain,
            ln_bias,
            w_in,
            b_in,
            w_out,
            b_out,
            layer_scale,
        )
    ]
    pad_shape = (tiles * (side + 2), side + 2 * OFF, channels)
    strip_shape = (tiles, side, 2 * OFF, channels)
    vector = pltpu.VMEM((1, channels), jnp.float32)
    buffers = [pltpu.VMEM((ROWS * side, 2 * channels), jnp.bfloat16)] * 2
    passed = pl.pallas_call(
        functools.partial(inner_kernel, sizes),
        out_shape=(
            pltpu.VMEM((tiles, side, side - 2 * OFF, channels), jnp.bfloat16),
            pltpu.VMEM(strip_shape, jnp.float32),
            pltpu.VMEM(pad_shape, jnp.float32),
            pltpu.VMEM((2 * channels, hidden), jnp.bfloat16),
            pltpu.VMEM((hidden, channels), jnp.bfloat16),
            pltpu.VMEM(dw_weight.shape, jnp.float32),
            vector,
            vector,
        ),
        in_specs=[anywhere] * len(operands),
        out_specs=(vmem,) * 8,
        scratch_shapes=[
            pltpu.VMEM(cells.shape, jnp.bfloat16),
            pltpu.VMEM((edges, side, channels), jnp.bfloat16),
            pltpu.VMEM((2 * CROSS, side, channels), jnp.bfloat16),
            pltpu.VMEM((2 * CROSS, side, channels), jnp.bfloat16),
            *buffers,
            pltpu.SMEM(tables[0].shape, jnp.int32),
            pltpu.SMEM(tables[1].shape, jnp.int32),
            vector,
            vector,
            pltpu.VMEM(w_in.shape, jnp.bfloat16),
            pltpu.VMEM(b_in.shape, jnp.bfloat16),
            pltpu.VMEM(w_out.shape, jnp.bfloat16),
            vector,
            vector,
            pltpu.SemaphoreType.DMA((tiles,)),
            pltpu.SemaphoreType.DMA((2,)),
            pltpu.SemaphoreType.DMA((9,)),
            pltpu.SemaphoreType.DMA((2,)),
            pltpu.SemaphoreType.DMA((2,)),
        ],
        compiler_params=pltpu.CompilerParams(
            collective_id=0, has_side_effects=True, vmem_limit_bytes=GRANT
        ),
        name="inner",
    )(*operands)
    return pl.pallas_call(
        edge_kernel,
        out_shape=(
            jax.ShapeDtypeStruct(cells.shape, jnp.bfloat16),
            pltpu.VMEM(strip_shape, jnp.float32),
        ),
        in_specs=[vmem] * 8,
        out_specs=(anywhere, vmem),
        input_output_aliases={1: 1},
        scratch_shapes=[
            pltpu.VMEM((tiles, 2, side, channels), jnp.bfloat16),
            pltpu.VMEM((tiles, 2, side, OFF, channels), jnp.bfloat16),
            *buffers,
            pltpu.SemaphoreType.DMA((tiles,)),
            pltpu.SemaphoreType.DMA((tiles, 2)),
            pltpu.SemaphoreType.DMA((tiles, 2)),
        ],
        compiler_params=pltpu.CompilerParams(vmem_limit_bytes=GRANT),
        name="edge",
    )(*passed)[0]


def solution(mesh):
    spread_spec = P(AXES, None, None, None)
    in_specs = (spread_spec, P(AXES, None), P(AXES, None)) + (P(),) * 9
    sizes = (mesh.shape["tile"], mesh.shape["hidden"])
    return jax.shard_map(
        functools.partial(per_device, sizes),
        mesh=mesh,
        in_specs=in_specs,
        out_specs=spread_spec,
        check_vma=False,
    )
```

```python
import functools

import jax
import jax.numpy as jnp
from jax import lax
from jax.experimental import pallas as pl
from jax.experimental.pallas import tpu as pltpu
from jax.sharding import PartitionSpec as P

AXES = ("tile", "hidden")
OFF = 8
ROWS = 8
UNROLL = 2
CROSS = 4
GRANT = 40 * 1024 * 1024
MESH = pl.DeviceIdType.MESH
ROOT_HALF = 0.7071067811865476


def tile_of(q, per_tile, tiles):
    tile = 0
    for j in range(1, tiles):
        tile = tile + jnp.where(q >= j * per_tile, 1, 0)
    return tile


def row_lines(pad_ref, side, tile, row):
    line = tile * (side + 2) + row
    return lambda a, b: pad_ref[line + a, pl.ds(OFF - 1 + b, side), :]


def col_lines(col_ref, side, tile, n):
    return lambda a, b: col_ref[tile, n, 2 - b if n else b, pl.ds(OFF - 1 + a, side), :]


def conv(dw_ref, dw_bias_ref, side, segments, dst):
    channels = dw_ref.shape[1]
    for n, load in enumerate(segments):
        total = jnp.broadcast_to(dw_bias_ref[...], (side, channels))
        for a in range(3):
            for b in range(3):
                total = total + dw_ref[3 * a + b : 3 * a + b + 1] * load(a, b)
        center = total - jnp.mean(total, axis=-1, keepdims=True)
        spread = jnp.sum(center * center, axis=-1, keepdims=True)
        value = center * lax.rsqrt(spread + 1e-06 * channels)
        dst[n * side : (n + 1) * side, 0:channels] = value.astype(jnp.bfloat16)


def mlp(w_aug_ref, w_fin_ref, bias_ref, side, segments, src):
    z = jnp.dot(src[...], w_aug_ref[...], preferred_element_type=jnp.float32)
    z = z.astype(jnp.bfloat16)
    act = z * (lax.erf(z) + jnp.bfloat16(1))
    mixed = jnp.dot(act, w_fin_ref[...], preferred_element_type=jnp.float32)
    for n, (load, store) in enumerate(segments):
        store(load(1, 1) + (mixed[n * side : (n + 1) * side] + bias_ref[...]))


def fill_ones(buf):
    rows, both = buf.shape
    lane = lax.broadcasted_iota(jnp.int32, (rows, both // 2), 1)
    buf[:, both // 2 :] = jnp.where(lane < 2, 1.0, 0.0).astype(jnp.bfloat16)


def last_flagged(flags, values):
    found = [jnp.int32(0)] * CROSS
    for flag, value in zip(flags, values):
        for k in range(CROSS - 1, 0, -1):
            found[k] = jnp.where(flag, found[k - 1], found[k])
        found[0] = jnp.where(flag, value, found[0])
    return found


def owned(partner, device, edges):
    local = partner - device * edges
    return (local >= 0) & (local < edges), local


def above(values, limit):
    return sum(jnp.where(value > limit, 1, 0) for value in values)


def split_bf16(value):
    high = value.astype(jnp.bfloat16).astype(jnp.float32)
    return high, value - high


def fold_weights(gain_ref, ln_bias_ref, w_in, b_in, w_out, b_out_ref, scale_ref, w_aug_ref, w_fin_ref, bias_ref):
    hidden, channels = w_in.shape
    eye = (
        lax.broadcasted_iota(jnp.int32, (channels, channels), 0)
        == lax.broadcasted_iota(jnp.int32, (channels, channels), 1)
    ).astype(jnp.bfloat16)
    gain = gain_ref[...] * (ROOT_HALF * channels**0.5)
    w_gain = (w_in.astype(jnp.float32) * gain).astype(jnp.bfloat16)
    turned = (((1,), (1,)), ((), ()))
    w_aug_ref[0:channels, :] = lax.dot_general(
        eye, w_gain, turned, preferred_element_type=jnp.float32
    ).astype(jnp.bfloat16)
    high, rest = split_bf16(ln_bias_ref[...])
    middle, low = split_bf16(rest)
    row_id = lax.broadcasted_iota(jnp.int32, (16, channels), 0)
    parts = jnp.where(
        row_id == 0, high, jnp.where(row_id == 1, middle, jnp.where(row_id == 2, low, 0.0))
    ).astype(jnp.bfloat16)
    moved = lax.dot_general(parts, w_in, turned, preferred_element_type=jnp.float32)
    moved = jnp.sum(moved, axis=0, keepdims=True)
    total = (b_in.astype(jnp.float32).reshape(1, hidden) + moved) * ROOT_HALF
    high, rest = split_bf16(total)
    row_id = lax.broadcasted_iota(jnp.int32, (channels, hidden), 0)
    extra = jnp.where(row_id == 0, high, jnp.where(row_id == 1, rest, 0.0))
    w_aug_ref[channels : 2 * channels, :] = extra.astype(jnp.bfloat16)
    scale = scale_ref[...]
    w_fin_ref[...] = (w_out.astype(jnp.float32) * (scale * ROOT_HALF)).astype(jnp.bfloat16)
    bias_ref[...] = scale * b_out_ref[...]


def inner_kernel(
    sizes,
    cells_ref,
    partner_hbm,
    flip_hbm,
    dw_hbm,
    dw_bias_hbm,
    gain_hbm,
    ln_bias_hbm,
    w_in_hbm,
    b_in_hbm,
    w_out_hbm,
    b_out_hbm,
    scale_hbm,
    mid_ref,
    strip_ref,
    pad_ref,
    col_ref,
    w_aug_ref,
    w_fin_ref,
    dw_ref,
    dw_bias_ref,
    bias_ref,
    mid_buf,
    side_buf,
    cap_buf,
    rims_ref,
    recv_ref,
    send_buf,
    buf_a,
    buf_b,
    partner_ref,
    flip_ref,
    gain_ref,
    ln_bias_ref,
    w_in_ref,
    b_in_ref,
    w_out_ref,
    b_out_ref,
    scale_ref,
    load_sem,
    cap_sem,
    side_sem,
    table_sem,
    weight_sem,
    send_sem,
    recv_sem,
):
    tile_devices, hidden_devices = sizes
    tiles, side, _, channels = cells_ref.shape
    edges = 4 * tiles
    width = side + 2 * OFF
    devices = tile_devices * hidden_devices
    me = lax.axis_index("tile") * hidden_devices + lax.axis_index("hidden")

    def at(position):
        return (position // hidden_devices, position % hidden_devices)

    right = lax.rem(me + 1, devices)
    left = lax.rem(me + devices - 1, devices)
    tables = [
        pltpu.make_async_copy(src, dst, table_sem.at[n])
        for n, (src, dst) in enumerate(((partner_hbm, partner_ref), (flip_hbm, flip_ref)))
    ]
    caps = [
        pltpu.make_async_copy(cells_ref.at[t, row], cap_buf.at[t, n], cap_sem.at[t, n])
        for t in range(tiles)
        for n, row in enumerate((0, side - 1))
    ]
    borders = [
        pltpu.make_async_copy(
            cells_ref.at[t, :, pl.ds(col, OFF)], side_buf.at[t, n], side_sem.at[t, n]
        )
        for t in range(tiles)
        for n, col in enumerate((0, side - OFF))
    ]
    mids = [
        pltpu.make_async_copy(
            cells_ref.at[t, :, pl.ds(OFF, side - 2 * OFF)], mid_buf.at[t], load_sem.at[t]
        )
        for t in range(tiles)
    ]
    weights = [
        pltpu.make_async_copy(src, dst, weight_sem.at[n])
        for n, (src, dst) in enumerate(
            (
                (w_in_hbm, w_in_ref),
                (w_out_hbm, w_out_ref),
                (b_in_hbm, b_in_ref),
                (gain_hbm, gain_ref),
                (ln_bias_hbm, ln_bias_ref),
                (b_out_hbm, b_out_ref),
                (scale_hbm, scale_ref),
                (dw_hbm, dw_ref),
                (dw_bias_hbm, dw_bias_ref),
            )
        )
    ]
    for copy in tables + caps + borders + weights + mids:
        copy.start()
    barrier = pltpu.get_barrier_semaphore()
    for neighbour in (left, right):
        pl.semaphore_signal(barrier, inc=1, device_id=at(neighbour), device_id_type=MESH)

    fill_ones(buf_a)
    fill_ones(buf_b)
    for copy in tables:
        copy.wait()
    partners = [partner_ref[e // 4, e % 4] for e in range(edges)]
    local = [jnp.int32(e) for e in range(edges)]
    going = []
    for device in (right, left):
        going += last_flagged([owned(p, device, edges)[0] for p in partners], local)

    def one_hot(found):
        return jnp.where(found, 1.0, 0.0).astype(jnp.bfloat16)

    r_id = lax.broadcasted_iota(jnp.int32, (side, side), 0)
    c_id = lax.broadcasted_iota(jnp.int32, (side, side), 1)
    along, against = c_id - r_id, c_id + r_id - (side - 1)
    r_id = lax.broadcasted_iota(jnp.int32, (side, side * OFF), 0)
    c_id = lax.broadcasted_iota(jnp.int32, (side, side * OFF), 1)
    far_along, far_against = c_id - OFF * r_id, c_id + OFF * r_id - OFF * (side - 1)
    for copy in caps + borders:
        copy.wait()
    for t in range(tiles):
        for s in range(4):
            flip = flip_ref[t, s] == 1
            if s % 2 == 0:
                order = one_hot(jnp.where(flip, against, along) == 0)
                source = cap_buf[t, s // 2]
            else:
                n = 1 - s // 2
                order = one_hot(jnp.where(flip, far_against, far_along) == n * (OFF - 1))
                source = side_buf[t, n].reshape(side * OFF, channels)
            rims_ref[4 * t + s] = jnp.dot(
                order, source, preferred_element_type=jnp.float32
            ).astype(jnp.bfloat16)
    for k in range(2 * CROSS):
        send_buf[k] = rims_ref[going[k]]

    sends = [
        pltpu.make_async_remote_copy(
            src_ref=send_buf.at[pl.ds(side_id * CROSS, CROSS)],
            dst_ref=recv_ref.at[pl.ds(side_id * CROSS, CROSS)],
            send_sem=send_sem.at[side_id],
            recv_sem=recv_sem.at[side_id],
            device_id=at(target),
            device_id_type=MESH,
        )
        for side_id, target in ((0, right), (1, left))
    ]

    def send():
        pl.semaphore_wait(barrier, 2)
        for copy in sends:
            copy.start()

    @pl.when(me == devices - 1)
    def _():
        send()

    for copy in weights:
        copy.wait()
    fold_weights(
        gain_ref,
        ln_bias_ref,
        w_in_ref[...],
        b_in_ref[...],
        w_out_ref[...],
        b_out_ref,
        scale_ref,
        w_aug_ref,
        w_fin_ref,
        bias_ref,
    )
    for t in range(tiles):
        rows = pl.ds(t * (side + 2) + 1, side)
        for n in range(2):
            line = side_buf[t, n]
            pad_ref[rows, pl.ds(OFF + n * (side - OFF), OFF), :] = line.astype(jnp.float32)
            for k in range(2):
                order = one_hot(far_along == (OFF - 1 - k if n else k))
                col_ref[t, n, k + 1, pl.ds(OFF, side), :] = jnp.dot(
                    order,
                    line.reshape(side * OFF, channels),
                    preferred_element_type=jnp.float32,
                )
    for t in range(tiles):
        mids[t].wait()
        rows = pl.ds(t * (side + 2) + 1, side)
        pad_ref[rows, pl.ds(2 * OFF, side - 2 * OFF), :] = mid_buf[t].astype(jnp.float32)

    inner_rows = side - 2

    def rows_of(chunk):
        found = []
        for k in range(ROWS):
            q = chunk * ROWS + k
            tile = tile_of(q, inner_rows, tiles)
            found.append((tile, q - inner_rows * tile + 1))
        return found

    def do_conv(chunk, dst):
        lines = [row_lines(pad_ref, side, tile, row) for tile, row in rows_of(chunk)]
        conv(dw_ref, dw_bias_ref, side, lines, dst)

    def put(tile, row):
        def store(new):
            mid_ref[tile, row] = new[OFF : side - OFF].astype(jnp.bfloat16)
            strip_ref[tile, row, 0:OFF, :] = new[:OFF]
            strip_ref[tile, row, OFF:, :] = new[side - OFF :]

        return store

    def do_mlp(chunk, src):
        lines = [
            (row_lines(pad_ref, side, tile, row), put(tile, row)) for tile, row in rows_of(chunk)
        ]
        mlp(w_aug_ref, w_fin_ref, bias_ref, side, lines, src)

    chunks = tiles * inner_rows // ROWS
    bufs = (buf_a, buf_b)
    do_conv(0, buf_a)
    rounds = (chunks - 1) // UNROLL
    turn = jnp.where(me == 0, rounds - 1, jnp.where(me == devices - 1, rounds, min(2, rounds - 1)))

    @pl.loop(0, rounds)
    def _(i):
        @pl.when(i == turn)
        def _():
            send()

        for u in range(UNROLL):
            do_mlp(UNROLL * i + u, bufs[u % 2])
            do_conv(UNROLL * i + u + 1, bufs[(u + 1) % 2])

    for c in range((chunks - 1) // UNROLL * UNROLL, chunks):
        do_mlp(c, bufs[c % 2])
        if c + 1 < chunks:
            do_conv(c + 1, bufs[(c + 1) % 2])
    for copy in sends:
        copy.wait()

    prev_flags, prev_local = zip(*[owned(p, left, edges) for p in partners])
    next_flags, next_local = zip(*[owned(p, right, edges) for p in partners])
    prev_list = last_flagged(prev_flags, prev_local)
    next_list = last_flagged(next_flags, next_local)
    for t in range(tiles):
        lines = []
        for s in range(4):
            e = 4 * t + s
            is_prev, is_next = prev_flags[e], next_flags[e]
            slot = jnp.where(
                is_prev,
                above(prev_list, prev_local[e]),
                CROSS + above(next_list, next_local[e]),
            )
            crosses = is_prev | is_next
            own_edge = jnp.clip(jnp.where(crosses, 0, partners[e] - me * edges), 0, edges - 1)
            received = recv_ref[jnp.clip(jnp.where(crosses, slot, 0), 0, 2 * CROSS - 1)]
            line = jnp.where(crosses, received, rims_ref[own_edge])
            lines.append(line.astype(jnp.float32))
        north, east, south, west = lines
        top = t * (side + 2)
        end = top + side + 1
        pad_ref[top, pl.ds(OFF, side), :] = north
        pad_ref[end, pl.ds(OFF, side), :] = south
        for n, line in enumerate((west, east)):
            col_ref[t, n, 0, pl.ds(OFF, side), :] = line
            inner = side - 1 if n else 0
            outer = pl.ds(OFF + side if n else OFF - 1, 1)
            pad_ref[top, outer, :] = 0.5 * (north[inner : inner + 1] + line[:1])
            pad_ref[end, outer, :] = 0.5 * (south[inner : inner + 1] + line[-1:])
            for row in (0, 1, side - 2, side - 1):
                pad_ref[top + 1 + row, outer, :] = line[row : row + 1]


def edge_kernel(
    mid_ref,
    strip_in_ref,
    pad_ref,
    col_ref,
    w_aug_ref,
    w_fin_ref,
    dw_ref,
    dw_bias_ref,
    bias_ref,
    out_hbm,
    strip_ref,
    caps_ref,
    sides_ref,
    buf_a,
    buf_b,
    mid_sem,
    cap_sem,
    side_sem,
):
    tiles, side, _, channels = out_hbm.shape
    mid_copies = [
        pltpu.make_async_copy(
            mid_ref.at[t, pl.ds(1, side - 2)],
            out_hbm.at[t, pl.ds(1, side - 2), pl.ds(OFF, side - 2 * OFF)],
            mid_sem.at[t],
        )
        for t in range(tiles)
    ]
    for copy in mid_copies:
        copy.start()
    fill_ones(buf_a)
    fill_ones(buf_b)
    flat_strip = strip_ref.reshape(tiles * side * 2 * OFF, channels)

    def put_cap(tile, n):
        def store(new):
            caps_ref[tile, n] = new.astype(jnp.bfloat16)

        return store

    def put_side(tile, n):
        first = tile * side * 2 * OFF + n * (2 * OFF - 1)

        def store(new):
            flat_strip[pl.ds(first, side, stride=2 * OFF), :] = new

        return store

    def lines_of(tile):
        return [
            (row_lines(pad_ref, side, tile, 0), put_cap(tile, 0)),
            (row_lines(pad_ref, side, tile, side - 1), put_cap(tile, 1)),
            (col_lines(col_ref, side, tile, 0), put_side(tile, 0)),
            (col_lines(col_ref, side, tile, 1), put_side(tile, 1)),
        ]

    groups = [
        [line for t in range(g, g + 2) for line in lines_of(t)] for g in range(0, tiles, 2)
    ]
    bufs = (buf_a, buf_b)
    copies = []

    def finish(g):
        for t in (2 * g, 2 * g + 1):
            for n, row in enumerate((0, side - 1)):
                copies.append(
                    pltpu.make_async_copy(
                        caps_ref.at[t, n], out_hbm.at[t, row], cap_sem.at[t, n]
                    )
                )
                copies[-1].start()
            for n, col in enumerate((0, side - OFF)):
                sides_ref[t, n] = strip_ref[t, :, n * OFF : (n + 1) * OFF, :].astype(jnp.bfloat16)
                copies.append(
                    pltpu.make_async_copy(
                        sides_ref.at[t, n, pl.ds(1, side - 2)],
                        out_hbm.at[t, pl.ds(1, side - 2), pl.ds(col, OFF)],
                        side_sem.at[t, n],
                    )
                )
                copies[-1].start()

    for g, group in enumerate(groups):
        conv(dw_ref, dw_bias_ref, side, [load for load, _ in group], bufs[g % 2])
        if g:
            mlp(w_aug_ref, w_fin_ref, bias_ref, side, groups[g - 1], bufs[(g - 1) % 2])
            finish(g - 1)
    mlp(w_aug_ref, w_fin_ref, bias_ref, side, groups[-1], bufs[(len(groups) - 1) % 2])
    finish(len(groups) - 1)
    for copy in mid_copies + copies:
        copy.wait()


def per_device(sizes, cells, *rest):
    tables, (dw_weight, dw_bias, ln_gain, ln_bias, w_in, b_in, w_out, b_out, layer_scale) = (
        rest[:2],
        rest[2:],
    )
    tiles, side, _, channels = cells.shape
    hidden = w_in.shape[0]
    edges = 4 * tiles
    vmem = pl.BlockSpec(memory_space=pltpu.VMEM)
    anywhere = pl.BlockSpec(memory_space=pltpu.HBM)
    dw_bias, ln_gain, ln_bias, b_out, layer_scale = (
        vector.reshape(1, channels)
        for vector in (dw_bias, ln_gain, ln_bias, b_out, layer_scale)
    )
    operands = [
        pltpu.with_memory_space_constraint(array, pltpu.HBM)
        for array in (
            cells,
            *tables,
            dw_weight,
            dw_bias,
            ln_gain,
            ln_bias,
            w_in,
            b_in,
            w_out,
            b_out,
            layer_scale,
        )
    ]
    pad_shape = (tiles * (side + 2), side + 2 * OFF, channels)
    strip_shape = (tiles, side, 2 * OFF, channels)
    vector = pltpu.VMEM((1, channels), jnp.float32)
    buffers = [pltpu.VMEM((ROWS * side, 2 * channels), jnp.bfloat16)] * 2
    passed = pl.pallas_call(
        functools.partial(inner_kernel, sizes),
        out_shape=(
            pltpu.VMEM((tiles, side, side - 2 * OFF, channels), jnp.bfloat16),
            pltpu.VMEM(strip_shape, jnp.float32),
            pltpu.VMEM(pad_shape, jnp.float32),
            pltpu.VMEM((tiles, 2, 3, side + 2 * OFF, channels), jnp.float32),
            pltpu.VMEM((2 * channels, hidden), jnp.bfloat16),
            pltpu.VMEM((hidden, channels), jnp.bfloat16),
            pltpu.VMEM(dw_weight.shape, jnp.float32),
            vector,
            vector,
        ),
        in_specs=[anywhere] * len(operands),
        out_specs=(vmem,) * 9,
        scratch_shapes=[
            pltpu.VMEM((tiles, side, side - 2 * OFF, channels), jnp.bfloat16),
            pltpu.VMEM((tiles, 2, side, OFF, channels), jnp.bfloat16),
            pltpu.VMEM((tiles, 2, side, channels), jnp.bfloat16),
            pltpu.VMEM((edges, side, channels), jnp.bfloat16),
            pltpu.VMEM((2 * CROSS, side, channels), jnp.bfloat16),
            pltpu.VMEM((2 * CROSS, side, channels), jnp.bfloat16),
            *buffers,
            pltpu.SMEM(tables[0].shape, jnp.int32),
            pltpu.SMEM(tables[1].shape, jnp.int32),
            vector,
            vector,
            pltpu.VMEM(w_in.shape, jnp.bfloat16),
            pltpu.VMEM(b_in.shape, jnp.bfloat16),
            pltpu.VMEM(w_out.shape, jnp.bfloat16),
            vector,
            vector,
            pltpu.SemaphoreType.DMA((tiles,)),
            pltpu.SemaphoreType.DMA((tiles, 2)),
            pltpu.SemaphoreType.DMA((tiles, 2)),
            pltpu.SemaphoreType.DMA((2,)),
            pltpu.SemaphoreType.DMA((9,)),
            pltpu.SemaphoreType.DMA((2,)),
            pltpu.SemaphoreType.DMA((2,)),
        ],
        compiler_params=pltpu.CompilerParams(
            collective_id=0, has_side_effects=True, vmem_limit_bytes=GRANT
        ),
        name="inner",
    )(*operands)
    return pl.pallas_call(
        edge_kernel,
        out_shape=(
            jax.ShapeDtypeStruct(cells.shape, jnp.bfloat16),
            pltpu.VMEM(strip_shape, jnp.float32),
        ),
        in_specs=[vmem] * 9,
        out_specs=(anywhere, vmem),
        input_output_aliases={1: 1},
        scratch_shapes=[
            pltpu.VMEM((tiles, 2, side, channels), jnp.bfloat16),
            pltpu.VMEM((tiles, 2, side, OFF, channels), jnp.bfloat16),
            *buffers,
            pltpu.SemaphoreType.DMA((tiles,)),
            pltpu.SemaphoreType.DMA((tiles, 2)),
            pltpu.SemaphoreType.DMA((tiles, 2)),
        ],
        compiler_params=pltpu.CompilerParams(vmem_limit_bytes=GRANT),
        name="edge",
    )(*passed)[0]


def solution(mesh):
    spread_spec = P(AXES, None, None, None)
    in_specs = (spread_spec, P(AXES, None), P(AXES, None)) + (P(),) * 9
    sizes = (mesh.shape["tile"], mesh.shape["hidden"])
    return jax.shard_map(
        functools.partial(per_device, sizes),
        mesh=mesh,
        in_specs=in_specs,
        out_specs=spread_spec,
        check_vma=False,
    )
```

```python
import functools

import jax
import jax.numpy as jnp
from jax import lax
from jax.experimental import pallas as pl
from jax.experimental.pallas import tpu as pltpu
from jax.sharding import PartitionSpec as P

AXES = ("tile", "hidden")
OFF = 8
ROWS = 8
UNROLL = 4
CROSS = 4
GRANT = 40 * 1024 * 1024
MESH = pl.DeviceIdType.MESH
ROOT_HALF = 0.7071067811865476


def tile_of(q, per_tile, tiles):
    tile = 0
    for j in range(1, tiles):
        tile = tile + jnp.where(q >= j * per_tile, 1, 0)
    return tile


def row_lines(pad_ref, side, tile, row):
    line = tile * (side + 2) + row
    return lambda a, b: pad_ref[line + a, pl.ds(OFF - 1 + b, side), :]


def col_lines(col_ref, side, tile, n):
    return lambda a, b: col_ref[tile, n, 2 - b if n else b, pl.ds(OFF - 1 + a, side), :]


def conv(dw_ref, dw_bias_ref, side, segments, dst):
    channels = dw_ref.shape[1]
    for n, load in enumerate(segments):
        total = jnp.broadcast_to(dw_bias_ref[...], (side, channels))
        for a in range(3):
            for b in range(3):
                total = total + dw_ref[3 * a + b : 3 * a + b + 1] * load(a, b)
        center = total - jnp.mean(total, axis=-1, keepdims=True)
        spread = jnp.sum(center * center, axis=-1, keepdims=True)
        value = center * lax.rsqrt(spread + 1e-06 * channels)
        dst[n * side : (n + 1) * side, 0:channels] = value.astype(jnp.bfloat16)


def mlp(w_aug_ref, w_fin_ref, bias_ref, side, segments, src):
    z = jnp.dot(src[...], w_aug_ref[...], preferred_element_type=jnp.float32)
    z = z.astype(jnp.bfloat16)
    act = z * (lax.erf(z) + jnp.bfloat16(1))
    mixed = jnp.dot(act, w_fin_ref[...], preferred_element_type=jnp.float32)
    for n, (load, store) in enumerate(segments):
        store(load(1, 1) + (mixed[n * side : (n + 1) * side] + bias_ref[...]))


def fill_ones(buf):
    rows, both = buf.shape
    lane = lax.broadcasted_iota(jnp.int32, (rows, both // 2), 1)
    buf[:, both // 2 :] = jnp.where(lane < 2, 1.0, 0.0).astype(jnp.bfloat16)


def last_flagged(flags, values):
    found = [jnp.int32(0)] * CROSS
    for flag, value in zip(flags, values):
        for k in range(CROSS - 1, 0, -1):
            found[k] = jnp.where(flag, found[k - 1], found[k])
        found[0] = jnp.where(flag, value, found[0])
    return found


def owned(partner, device, edges):
    local = partner - device * edges
    return (local >= 0) & (local < edges), local


def above(values, limit):
    return sum(jnp.where(value > limit, 1, 0) for value in values)


def split_bf16(value):
    high = value.astype(jnp.bfloat16).astype(jnp.float32)
    return high, value - high


def fold_weights(gain_ref, ln_bias_ref, w_in, b_in, w_out, b_out_ref, scale_ref, w_aug_ref, w_fin_ref, bias_ref):
    hidden, channels = w_in.shape
    eye = (
        lax.broadcasted_iota(jnp.int32, (channels, channels), 0)
        == lax.broadcasted_iota(jnp.int32, (channels, channels), 1)
    ).astype(jnp.bfloat16)
    gain = gain_ref[...] * (ROOT_HALF * channels**0.5)
    w_gain = (w_in.astype(jnp.float32) * gain).astype(jnp.bfloat16)
    turned = (((1,), (1,)), ((), ()))
    w_aug_ref[0:channels, :] = lax.dot_general(
        eye, w_gain, turned, preferred_element_type=jnp.float32
    ).astype(jnp.bfloat16)
    high, rest = split_bf16(ln_bias_ref[...])
    middle, low = split_bf16(rest)
    row_id = lax.broadcasted_iota(jnp.int32, (16, channels), 0)
    parts = jnp.where(
        row_id == 0, high, jnp.where(row_id == 1, middle, jnp.where(row_id == 2, low, 0.0))
    ).astype(jnp.bfloat16)
    moved = lax.dot_general(parts, w_in, turned, preferred_element_type=jnp.float32)
    moved = jnp.sum(moved, axis=0, keepdims=True)
    total = (b_in.astype(jnp.float32).reshape(1, hidden) + moved) * ROOT_HALF
    high, rest = split_bf16(total)
    row_id = lax.broadcasted_iota(jnp.int32, (channels, hidden), 0)
    extra = jnp.where(row_id == 0, high, jnp.where(row_id == 1, rest, 0.0))
    w_aug_ref[channels : 2 * channels, :] = extra.astype(jnp.bfloat16)
    scale = scale_ref[...]
    w_fin_ref[...] = (w_out.astype(jnp.float32) * (scale * ROOT_HALF)).astype(jnp.bfloat16)
    bias_ref[...] = scale * b_out_ref[...]


def inner_kernel(
    sizes,
    cells_ref,
    partner_hbm,
    flip_hbm,
    dw_hbm,
    dw_bias_hbm,
    gain_hbm,
    ln_bias_hbm,
    w_in_hbm,
    b_in_hbm,
    w_out_hbm,
    b_out_hbm,
    scale_hbm,
    mid_ref,
    strip_ref,
    pad_ref,
    col_ref,
    w_aug_ref,
    w_fin_ref,
    dw_ref,
    dw_bias_ref,
    bias_ref,
    mid_buf,
    side_buf,
    cap_buf,
    rims_ref,
    recv_ref,
    send_buf,
    buf_a,
    buf_b,
    partner_ref,
    flip_ref,
    gain_ref,
    ln_bias_ref,
    w_in_ref,
    b_in_ref,
    w_out_ref,
    b_out_ref,
    scale_ref,
    load_sem,
    cap_sem,
    side_sem,
    table_sem,
    weight_sem,
    send_sem,
    recv_sem,
):
    tile_devices, hidden_devices = sizes
    tiles, side, _, channels = cells_ref.shape
    edges = 4 * tiles
    width = side + 2 * OFF
    devices = tile_devices * hidden_devices
    me = lax.axis_index("tile") * hidden_devices + lax.axis_index("hidden")

    def at(position):
        return (position // hidden_devices, position % hidden_devices)

    right = lax.rem(me + 1, devices)
    left = lax.rem(me + devices - 1, devices)
    tables = [
        pltpu.make_async_copy(src, dst, table_sem.at[n])
        for n, (src, dst) in enumerate(((partner_hbm, partner_ref), (flip_hbm, flip_ref)))
    ]
    caps = [
        pltpu.make_async_copy(cells_ref.at[t, row], cap_buf.at[t, n], cap_sem.at[t, n])
        for t in range(tiles)
        for n, row in enumerate((0, side - 1))
    ]
    borders = [
        pltpu.make_async_copy(
            cells_ref.at[t, :, pl.ds(col, OFF)], side_buf.at[t, n], side_sem.at[t, n]
        )
        for t in range(tiles)
        for n, col in enumerate((0, side - OFF))
    ]
    mids = [
        pltpu.make_async_copy(
            cells_ref.at[t, :, pl.ds(OFF, side - 2 * OFF)], mid_buf.at[t], load_sem.at[t]
        )
        for t in range(tiles)
    ]
    weights = [
        pltpu.make_async_copy(src, dst, weight_sem.at[n])
        for n, (src, dst) in enumerate(
            (
                (w_in_hbm, w_in_ref),
                (w_out_hbm, w_out_ref),
                (b_in_hbm, b_in_ref),
                (gain_hbm, gain_ref),
                (ln_bias_hbm, ln_bias_ref),
                (b_out_hbm, b_out_ref),
                (scale_hbm, scale_ref),
                (dw_hbm, dw_ref),
                (dw_bias_hbm, dw_bias_ref),
            )
        )
    ]
    for copy in tables + caps + borders + weights + mids:
        copy.start()
    barrier = pltpu.get_barrier_semaphore()
    for neighbour in (left, right):
        pl.semaphore_signal(barrier, inc=1, device_id=at(neighbour), device_id_type=MESH)

    fill_ones(buf_a)
    fill_ones(buf_b)
    for copy in tables:
        copy.wait()
    partners = [partner_ref[e // 4, e % 4] for e in range(edges)]
    local = [jnp.int32(e) for e in range(edges)]
    going = []
    for device in (right, left):
        going += last_flagged([owned(p, device, edges)[0] for p in partners], local)

    def one_hot(found):
        return jnp.where(found, 1.0, 0.0).astype(jnp.bfloat16)

    r_id = lax.broadcasted_iota(jnp.int32, (side, side), 0)
    c_id = lax.broadcasted_iota(jnp.int32, (side, side), 1)
    along, against = c_id - r_id, c_id + r_id - (side - 1)
    r_id = lax.broadcasted_iota(jnp.int32, (side, side * OFF), 0)
    c_id = lax.broadcasted_iota(jnp.int32, (side, side * OFF), 1)
    far_along, far_against = c_id - OFF * r_id, c_id + OFF * r_id - OFF * (side - 1)
    for copy in caps + borders:
        copy.wait()
    for t in range(tiles):
        for s in range(4):
            flip = flip_ref[t, s] == 1
            if s % 2 == 0:
                order = one_hot(jnp.where(flip, against, along) == 0)
                source = cap_buf[t, s // 2]
            else:
                n = 1 - s // 2
                order = one_hot(jnp.where(flip, far_against, far_along) == n * (OFF - 1))
                source = side_buf[t, n].reshape(side * OFF, channels)
            rims_ref[4 * t + s] = jnp.dot(
                order, source, preferred_element_type=jnp.float32
            ).astype(jnp.bfloat16)
    for k in range(2 * CROSS):
        send_buf[k] = rims_ref[going[k]]

    sends = [
        pltpu.make_async_remote_copy(
            src_ref=send_buf.at[pl.ds(side_id * CROSS, CROSS)],
            dst_ref=recv_ref.at[pl.ds(side_id * CROSS, CROSS)],
            send_sem=send_sem.at[side_id],
            recv_sem=recv_sem.at[side_id],
            device_id=at(target),
            device_id_type=MESH,
        )
        for side_id, target in ((0, right), (1, left))
    ]

    def send():
        pl.semaphore_wait(barrier, 2)
        for copy in sends:
            copy.start()

    @pl.when(me == devices - 1)
    def _():
        send()

    for copy in weights:
        copy.wait()
    fold_weights(
        gain_ref,
        ln_bias_ref,
        w_in_ref[...],
        b_in_ref[...],
        w_out_ref[...],
        b_out_ref,
        scale_ref,
        w_aug_ref,
        w_fin_ref,
        bias_ref,
    )
    for t in range(tiles):
        rows = pl.ds(t * (side + 2) + 1, side)
        for n in range(2):
            line = side_buf[t, n]
            pad_ref[rows, pl.ds(OFF + n * (side - OFF), OFF), :] = line.astype(jnp.float32)
            for k in range(2):
                order = one_hot(far_along == (OFF - 1 - k if n else k))
                col_ref[t, n, k + 1, pl.ds(OFF, side), :] = jnp.dot(
                    order,
                    line.reshape(side * OFF, channels),
                    preferred_element_type=jnp.float32,
                )
    for t in range(tiles):
        mids[t].wait()
        rows = pl.ds(t * (side + 2) + 1, side)
        pad_ref[rows, pl.ds(2 * OFF, side - 2 * OFF), :] = mid_buf[t].astype(jnp.float32)

    inner_rows = side - 2

    def rows_of(chunk):
        found = []
        for k in range(ROWS):
            q = chunk * ROWS + k
            tile = tile_of(q, inner_rows, tiles)
            found.append((tile, q - inner_rows * tile + 1))
        return found

    def do_conv(chunk, dst):
        lines = [row_lines(pad_ref, side, tile, row) for tile, row in rows_of(chunk)]
        conv(dw_ref, dw_bias_ref, side, lines, dst)

    def put(tile, row):
        def store(new):
            mid_ref[tile, row] = new[OFF : side - OFF].astype(jnp.bfloat16)
            strip_ref[tile, row, 0:OFF, :] = new[:OFF]
            strip_ref[tile, row, OFF:, :] = new[side - OFF :]

        return store

    def do_mlp(chunk, src):
        lines = [
            (row_lines(pad_ref, side, tile, row), put(tile, row)) for tile, row in rows_of(chunk)
        ]
        mlp(w_aug_ref, w_fin_ref, bias_ref, side, lines, src)

    chunks = tiles * inner_rows // ROWS
    bufs = (buf_a, buf_b)
    do_conv(0, buf_a)
    rounds = (chunks - 1) // UNROLL
    turn = jnp.where(me == 0, rounds - 1, jnp.where(me == devices - 1, rounds, min(1, rounds - 1)))

    @pl.loop(0, rounds)
    def _(i):
        @pl.when(i == turn)
        def _():
            send()

        for u in range(UNROLL):
            do_mlp(UNROLL * i + u, bufs[u % 2])
            do_conv(UNROLL * i + u + 1, bufs[(u + 1) % 2])

    for c in range((chunks - 1) // UNROLL * UNROLL, chunks):
        do_mlp(c, bufs[c % 2])
        if c + 1 < chunks:
            do_conv(c + 1, bufs[(c + 1) % 2])
    for copy in sends:
        copy.wait()

    prev_flags, prev_local = zip(*[owned(p, left, edges) for p in partners])
    next_flags, next_local = zip(*[owned(p, right, edges) for p in partners])
    prev_list = last_flagged(prev_flags, prev_local)
    next_list = last_flagged(next_flags, next_local)
    for t in range(tiles):
        lines = []
        for s in range(4):
            e = 4 * t + s
            is_prev, is_next = prev_flags[e], next_flags[e]
            slot = jnp.where(
                is_prev,
                above(prev_list, prev_local[e]),
                CROSS + above(next_list, next_local[e]),
            )
            crosses = is_prev | is_next
            own_edge = jnp.clip(jnp.where(crosses, 0, partners[e] - me * edges), 0, edges - 1)
            received = recv_ref[jnp.clip(jnp.where(crosses, slot, 0), 0, 2 * CROSS - 1)]
            line = jnp.where(crosses, received, rims_ref[own_edge])
            lines.append(line.astype(jnp.float32))
        north, east, south, west = lines
        top = t * (side + 2)
        end = top + side + 1
        pad_ref[top, pl.ds(OFF, side), :] = north
        pad_ref[end, pl.ds(OFF, side), :] = south
        for n, line in enumerate((west, east)):
            col_ref[t, n, 0, pl.ds(OFF, side), :] = line
            inner = side - 1 if n else 0
            outer = pl.ds(OFF + side if n else OFF - 1, 1)
            pad_ref[top, outer, :] = 0.5 * (north[inner : inner + 1] + line[:1])
            pad_ref[end, outer, :] = 0.5 * (south[inner : inner + 1] + line[-1:])
            for row in (0, 1, side - 2, side - 1):
                pad_ref[top + 1 + row, outer, :] = line[row : row + 1]


def edge_kernel(
    mid_ref,
    strip_in_ref,
    pad_ref,
    col_ref,
    w_aug_ref,
    w_fin_ref,
    dw_ref,
    dw_bias_ref,
    bias_ref,
    out_hbm,
    strip_ref,
    caps_ref,
    sides_ref,
    buf_a,
    buf_b,
    mid_sem,
    cap_sem,
    side_sem,
):
    tiles, side, _, channels = out_hbm.shape
    mid_copies = [
        pltpu.make_async_copy(
            mid_ref.at[t, pl.ds(1, side - 2)],
            out_hbm.at[t, pl.ds(1, side - 2), pl.ds(OFF, side - 2 * OFF)],
            mid_sem.at[t],
        )
        for t in range(tiles)
    ]
    for copy in mid_copies:
        copy.start()
    fill_ones(buf_a)
    fill_ones(buf_b)
    flat_strip = strip_ref.reshape(tiles * side * 2 * OFF, channels)

    def put_cap(tile, n):
        def store(new):
            caps_ref[tile, n] = new.astype(jnp.bfloat16)

        return store

    def put_side(tile, n):
        first = tile * side * 2 * OFF + n * (2 * OFF - 1)

        def store(new):
            flat_strip[pl.ds(first, side, stride=2 * OFF), :] = new

        return store

    def lines_of(tile):
        return [
            (row_lines(pad_ref, side, tile, 0), put_cap(tile, 0)),
            (row_lines(pad_ref, side, tile, side - 1), put_cap(tile, 1)),
            (col_lines(col_ref, side, tile, 0), put_side(tile, 0)),
            (col_lines(col_ref, side, tile, 1), put_side(tile, 1)),
        ]

    groups = [
        [line for t in range(g, g + 2) for line in lines_of(t)] for g in range(0, tiles, 2)
    ]
    bufs = (buf_a, buf_b)
    copies = []

    def finish(g):
        for t in (2 * g, 2 * g + 1):
            for n, row in enumerate((0, side - 1)):
                copies.append(
                    pltpu.make_async_copy(
                        caps_ref.at[t, n], out_hbm.at[t, row], cap_sem.at[t, n]
                    )
                )
                copies[-1].start()
            for n, col in enumerate((0, side - OFF)):
                sides_ref[t, n] = strip_ref[t, :, n * OFF : (n + 1) * OFF, :].astype(jnp.bfloat16)
                copies.append(
                    pltpu.make_async_copy(
                        sides_ref.at[t, n, pl.ds(1, side - 2)],
                        out_hbm.at[t, pl.ds(1, side - 2), pl.ds(col, OFF)],
                        side_sem.at[t, n],
                    )
                )
                copies[-1].start()

    for g, group in enumerate(groups):
        conv(dw_ref, dw_bias_ref, side, [load for load, _ in group], bufs[g % 2])
        if g:
            mlp(w_aug_ref, w_fin_ref, bias_ref, side, groups[g - 1], bufs[(g - 1) % 2])
            finish(g - 1)
    mlp(w_aug_ref, w_fin_ref, bias_ref, side, groups[-1], bufs[(len(groups) - 1) % 2])
    finish(len(groups) - 1)
    for copy in mid_copies + copies:
        copy.wait()


def per_device(sizes, cells, *rest):
    tables, (dw_weight, dw_bias, ln_gain, ln_bias, w_in, b_in, w_out, b_out, layer_scale) = (
        rest[:2],
        rest[2:],
    )
    tiles, side, _, channels = cells.shape
    hidden = w_in.shape[0]
    edges = 4 * tiles
    vmem = pl.BlockSpec(memory_space=pltpu.VMEM)
    anywhere = pl.BlockSpec(memory_space=pltpu.HBM)
    dw_bias, ln_gain, ln_bias, b_out, layer_scale = (
        vector.reshape(1, channels)
        for vector in (dw_bias, ln_gain, ln_bias, b_out, layer_scale)
    )
    operands = [
        pltpu.with_memory_space_constraint(array, pltpu.HBM)
        for array in (
            cells,
            *tables,
            dw_weight,
            dw_bias,
            ln_gain,
            ln_bias,
            w_in,
            b_in,
            w_out,
            b_out,
            layer_scale,
        )
    ]
    pad_shape = (tiles * (side + 2), side + 2 * OFF, channels)
    strip_shape = (tiles, side, 2 * OFF, channels)
    vector = pltpu.VMEM((1, channels), jnp.float32)
    buffers = [pltpu.VMEM((ROWS * side, 2 * channels), jnp.bfloat16)] * 2
    passed = pl.pallas_call(
        functools.partial(inner_kernel, sizes),
        out_shape=(
            pltpu.VMEM((tiles, side, side - 2 * OFF, channels), jnp.bfloat16),
            pltpu.VMEM(strip_shape, jnp.float32),
            pltpu.VMEM(pad_shape, jnp.float32),
            pltpu.VMEM((tiles, 2, 3, side + 2 * OFF, channels), jnp.float32),
            pltpu.VMEM((2 * channels, hidden), jnp.bfloat16),
            pltpu.VMEM((hidden, channels), jnp.bfloat16),
            pltpu.VMEM(dw_weight.shape, jnp.float32),
            vector,
            vector,
        ),
        in_specs=[anywhere] * len(operands),
        out_specs=(vmem,) * 9,
        scratch_shapes=[
            pltpu.VMEM((tiles, side, side - 2 * OFF, channels), jnp.bfloat16),
            pltpu.VMEM((tiles, 2, side, OFF, channels), jnp.bfloat16),
            pltpu.VMEM((tiles, 2, side, channels), jnp.bfloat16),
            pltpu.VMEM((edges, side, channels), jnp.bfloat16),
            pltpu.VMEM((2 * CROSS, side, channels), jnp.bfloat16),
            pltpu.VMEM((2 * CROSS, side, channels), jnp.bfloat16),
            *buffers,
            pltpu.SMEM(tables[0].shape, jnp.int32),
            pltpu.SMEM(tables[1].shape, jnp.int32),
            vector,
            vector,
            pltpu.VMEM(w_in.shape, jnp.bfloat16),
            pltpu.VMEM(b_in.shape, jnp.bfloat16),
            pltpu.VMEM(w_out.shape, jnp.bfloat16),
            vector,
            vector,
            pltpu.SemaphoreType.DMA((tiles,)),
            pltpu.SemaphoreType.DMA((tiles, 2)),
            pltpu.SemaphoreType.DMA((tiles, 2)),
            pltpu.SemaphoreType.DMA((2,)),
            pltpu.SemaphoreType.DMA((9,)),
            pltpu.SemaphoreType.DMA((2,)),
            pltpu.SemaphoreType.DMA((2,)),
        ],
        compiler_params=pltpu.CompilerParams(
            collective_id=0, has_side_effects=True, vmem_limit_bytes=GRANT
        ),
        name="inner",
    )(*operands)
    return pl.pallas_call(
        edge_kernel,
        out_shape=(
            jax.ShapeDtypeStruct(cells.shape, jnp.bfloat16),
            pltpu.VMEM(strip_shape, jnp.float32),
        ),
        in_specs=[vmem] * 9,
        out_specs=(anywhere, vmem),
        input_output_aliases={1: 1},
        scratch_shapes=[
            pltpu.VMEM((tiles, 2, side, channels), jnp.bfloat16),
            pltpu.VMEM((tiles, 2, side, OFF, channels), jnp.bfloat16),
            *buffers,
            pltpu.SemaphoreType.DMA((tiles,)),
            pltpu.SemaphoreType.DMA((tiles, 2)),
            pltpu.SemaphoreType.DMA((tiles, 2)),
        ],
        compiler_params=pltpu.CompilerParams(vmem_limit_bytes=GRANT),
        name="edge",
    )(*passed)[0]


def solution(mesh):
    spread_spec = P(AXES, None, None, None)
    in_specs = (spread_spec, P(AXES, None), P(AXES, None)) + (P(),) * 9
    sizes = (mesh.shape["tile"], mesh.shape["hidden"])
    return jax.shard_map(
        functools.partial(per_device, sizes),
        mesh=mesh,
        in_specs=in_specs,
        out_specs=spread_spec,
        check_vma=False,
    )
```

```python
import functools

import jax
import jax.numpy as jnp
from jax import lax
from jax.experimental import pallas as pl
from jax.experimental.pallas import tpu as pltpu
from jax.sharding import PartitionSpec as P

AXES = ("tile", "hidden")
OFF = 8
ROWS = 8
UNROLL = 6
CROSS = 4
GRANT = 40 * 1024 * 1024
MESH = pl.DeviceIdType.MESH
ROOT_HALF = 0.7071067811865476


def tile_of(q, per_tile, tiles):
    tile = 0
    for j in range(1, tiles):
        tile = tile + jnp.where(q >= j * per_tile, 1, 0)
    return tile


def rim_lines(line_ref, length, tile, s):
    def load(a, b):
        across, along = (a, b) if s % 2 == 0 else (b, a)
        return line_ref[tile, s, across if s in (0, 3) else 2 - across, pl.ds(OFF - 1 + along, length), :]

    return load


def normed(total, eps):
    center = total - jnp.mean(total, axis=-1, keepdims=True)
    spread = jnp.sum(center * center, axis=-1, keepdims=True)
    return (center * lax.rsqrt(spread + eps)).astype(jnp.bfloat16)


def conv(dw_ref, dw_bias_ref, side, segments, dst):
    channels = dw_ref.shape[1]
    for n, load in enumerate(segments):
        total = jnp.broadcast_to(dw_bias_ref[...], (side, channels))
        for a in range(3):
            for b in range(3):
                total = total + dw_ref[3 * a + b : 3 * a + b + 1] * load(a, b)
        dst[n * side : (n + 1) * side, 0:channels] = normed(total, 1e-06 * channels)


def whole_line(cells_buf, tile, row):
    side, step = cells_buf.shape[2], 2 * OFF
    return jnp.concatenate(
        [cells_buf[tile, row, n : n + step] for n in range(0, side, step)], axis=0
    )


def conv_rows(dw_ref, dw_bias_ref, cells_buf, shift_ref, rows, dst):
    side, channels = cells_buf.shape[2:]
    taps = [
        jnp.broadcast_to(dw_ref[k : k + 1], (side, channels)).astype(jnp.bfloat16)
        for k in range(9)
    ]
    for n, (tile, row) in enumerate(rows):
        lines = [
            whole_line(cells_buf, tile, row - 1 + a) for a in range(3)
        ]
        sums = []
        for b in range(3):
            part = taps[b] * lines[0]
            for a in range(1, 3):
                part = part + taps[3 * a + b] * lines[a]
            sums.append(part.astype(jnp.float32))
        shift_ref[n, 0, pl.ds(OFF, side), :] = sums[0]
        shift_ref[n, 1, pl.ds(OFF, side), :] = sums[2]
        total = (sums[1] + dw_bias_ref[...]) + (
            shift_ref[n, 0, pl.ds(OFF - 1, side), :] + shift_ref[n, 1, pl.ds(OFF + 1, side), :]
        )
        dst[n * side : (n + 1) * side, 0:channels] = normed(total, 1e-06 * channels)


def mlp(w_aug_ref, w_fin_ref, bias_ref, side, segments, src):
    z = jnp.dot(src[...], w_aug_ref[...], preferred_element_type=jnp.float32)
    z = z.astype(jnp.bfloat16)
    act = z * (lax.erf(z) + jnp.bfloat16(1))
    mixed = jnp.dot(act, w_fin_ref[...], preferred_element_type=jnp.float32)
    for n, (load, store) in enumerate(segments):
        store(load(1, 1).astype(jnp.float32) + (mixed[n * side : (n + 1) * side] + bias_ref[...]))


def fill_ones(buf):
    rows, both = buf.shape
    lane = lax.broadcasted_iota(jnp.int32, (rows, both // 2), 1)
    buf[:, both // 2 :] = jnp.where(lane < 2, 1.0, 0.0).astype(jnp.bfloat16)


def last_flagged(flags, values):
    found = [jnp.int32(0)] * CROSS
    for flag, value in zip(flags, values):
        for k in range(CROSS - 1, 0, -1):
            found[k] = jnp.where(flag, found[k - 1], found[k])
        found[0] = jnp.where(flag, value, found[0])
    return found


def owned(partner, device, edges):
    local = partner - device * edges
    return (local >= 0) & (local < edges), local


def above(values, limit):
    return sum(jnp.where(value > limit, 1, 0) for value in values)


def split_bf16(value):
    high = value.astype(jnp.bfloat16).astype(jnp.float32)
    return high, value - high


def fold_weights(gain_ref, ln_bias_ref, w_in, b_in, w_out, b_out_ref, scale_ref, w_aug_ref, w_fin_ref, bias_ref):
    hidden, channels = w_in.shape
    eye = (
        lax.broadcasted_iota(jnp.int32, (channels, channels), 0)
        == lax.broadcasted_iota(jnp.int32, (channels, channels), 1)
    ).astype(jnp.bfloat16)
    gain = gain_ref[...] * (ROOT_HALF * channels**0.5)
    w_gain = (w_in.astype(jnp.float32) * gain).astype(jnp.bfloat16)
    turned = (((1,), (1,)), ((), ()))
    w_aug_ref[0:channels, :] = lax.dot_general(
        eye, w_gain, turned, preferred_element_type=jnp.float32
    ).astype(jnp.bfloat16)
    high, rest = split_bf16(ln_bias_ref[...])
    middle, low = split_bf16(rest)
    row_id = lax.broadcasted_iota(jnp.int32, (16, channels), 0)
    parts = jnp.where(
        row_id == 0, high, jnp.where(row_id == 1, middle, jnp.where(row_id == 2, low, 0.0))
    ).astype(jnp.bfloat16)
    moved = lax.dot_general(parts, w_in, turned, preferred_element_type=jnp.float32)
    moved = jnp.sum(moved, axis=0, keepdims=True)
    total = (b_in.astype(jnp.float32).reshape(1, hidden) + moved) * ROOT_HALF
    high, rest = split_bf16(total)
    row_id = lax.broadcasted_iota(jnp.int32, (channels, hidden), 0)
    extra = jnp.where(row_id == 0, high, jnp.where(row_id == 1, rest, 0.0))
    w_aug_ref[channels : 2 * channels, :] = extra.astype(jnp.bfloat16)
    scale = scale_ref[...]
    w_fin_ref[...] = (w_out.astype(jnp.float32) * (scale * ROOT_HALF)).astype(jnp.bfloat16)
    bias_ref[...] = scale * b_out_ref[...]


def inner_kernel(
    sizes,
    cells_ref,
    partner_hbm,
    flip_hbm,
    dw_hbm,
    dw_bias_hbm,
    gain_hbm,
    ln_bias_hbm,
    w_in_hbm,
    b_in_hbm,
    w_out_hbm,
    b_out_hbm,
    scale_hbm,
    mid_ref,
    strip_ref,
    line_ref,
    w_aug_ref,
    w_fin_ref,
    dw_ref,
    dw_bias_ref,
    bias_ref,
    cells_buf,
    side_buf,
    cap_buf,
    rims_ref,
    recv_ref,
    send_buf,
    buf_a,
    buf_b,
    shift_ref,
    partner_ref,
    flip_ref,
    gain_ref,
    ln_bias_ref,
    w_in_ref,
    b_in_ref,
    w_out_ref,
    b_out_ref,
    scale_ref,
    load_sem,
    cap_sem,
    side_sem,
    table_sem,
    weight_sem,
    send_sem,
    recv_sem,
):
    tile_devices, hidden_devices = sizes
    tiles, side, _, channels = cells_ref.shape
    edges = 4 * tiles
    devices = tile_devices * hidden_devices
    me = lax.axis_index("tile") * hidden_devices + lax.axis_index("hidden")

    def at(position):
        return (position // hidden_devices, position % hidden_devices)

    right = lax.rem(me + 1, devices)
    left = lax.rem(me + devices - 1, devices)
    tables = [
        pltpu.make_async_copy(src, dst, table_sem.at[n])
        for n, (src, dst) in enumerate(((partner_hbm, partner_ref), (flip_hbm, flip_ref)))
    ]
    caps = [
        pltpu.make_async_copy(cells_ref.at[t, row], cap_buf.at[t, n], cap_sem.at[t, n])
        for t in range(tiles)
        for n, row in enumerate((0, side - 1))
    ]
    borders = [
        pltpu.make_async_copy(
            cells_ref.at[t, :, pl.ds(col, OFF)], side_buf.at[t, n], side_sem.at[t, n]
        )
        for t in range(tiles)
        for n, col in enumerate((0, side - OFF))
    ]
    loads = [
        pltpu.make_async_copy(cells_ref.at[t], cells_buf.at[t], load_sem.at[t])
        for t in range(tiles)
    ]
    weights = [
        pltpu.make_async_copy(src, dst, weight_sem.at[n])
        for n, (src, dst) in enumerate(
            (
                (w_in_hbm, w_in_ref),
                (w_out_hbm, w_out_ref),
                (b_in_hbm, b_in_ref),
                (gain_hbm, gain_ref),
                (ln_bias_hbm, ln_bias_ref),
                (b_out_hbm, b_out_ref),
                (scale_hbm, scale_ref),
                (dw_hbm, dw_ref),
                (dw_bias_hbm, dw_bias_ref),
            )
        )
    ]
    for copy in tables + weights + caps + borders + loads:
        copy.start()
    barrier = pltpu.get_barrier_semaphore()
    for neighbour in (left, right):
        pl.semaphore_signal(barrier, inc=1, device_id=at(neighbour), device_id_type=MESH)

    fill_ones(buf_a)
    fill_ones(buf_b)
    for copy in tables:
        copy.wait()
    for copy in weights:
        copy.wait()
    fold_weights(
        gain_ref,
        ln_bias_ref,
        w_in_ref[...],
        b_in_ref[...],
        w_out_ref[...],
        b_out_ref,
        scale_ref,
        w_aug_ref,
        w_fin_ref,
        bias_ref,
    )

    def one_hot(found):
        return jnp.where(found, 1.0, 0.0).astype(jnp.bfloat16)

    r_id = lax.broadcasted_iota(jnp.int32, (side, side), 0)
    c_id = lax.broadcasted_iota(jnp.int32, (side, side), 1)
    backward = one_hot(c_id + r_id == side - 1)
    r_id = lax.broadcasted_iota(jnp.int32, (side, side * OFF), 0)
    c_id = lax.broadcasted_iota(jnp.int32, (side, side * OFF), 1)
    picks = [
        jnp.concatenate(
            [one_hot(c_id - OFF * r_id == (OFF - 1 - k if n else k)) for k in range(2)], axis=0
        )
        for n in range(2)
    ]
    for copy in caps + borders:
        copy.wait()
    partners = [partner_ref[e // 4, e % 4] for e in range(edges)]
    local = [jnp.int32(e) for e in range(edges)]
    going = []
    for device in (right, left):
        going += last_flagged([owned(p, device, edges)[0] for p in partners], local)

    prev_flags, prev_local = zip(*[owned(p, left, edges) for p in partners])
    next_flags, next_local = zip(*[owned(p, right, edges) for p in partners])
    prev_list = last_flagged(prev_flags, prev_local)
    next_list = last_flagged(next_flags, next_local)
    halo_source = []
    for e in range(edges):
        slot = jnp.where(
            prev_flags[e],
            above(prev_list, prev_local[e]),
            CROSS + above(next_list, next_local[e]),
        )
        crosses = prev_flags[e] | next_flags[e]
        own_edge = jnp.clip(jnp.where(crosses, 0, partners[e] - me * edges), 0, edges - 1)
        slot = jnp.clip(jnp.where(crosses, slot, 0), 0, 2 * CROSS - 1)
        halo_source.append((crosses, slot, own_edge))

    lines = {}
    for n, s in enumerate((3, 1)):
        both = jnp.dot(
            picks[n],
            jnp.concatenate(
                [side_buf[t, n].reshape(side * OFF, channels) for t in range(tiles)], axis=1
            ),
            preferred_element_type=jnp.float32,
        )
        for t in range(tiles):
            part = both[:, t * channels : (t + 1) * channels]
            for k in range(2):
                line_ref[t, s, k + 1, pl.ds(OFF, side), :] = part[k * side : (k + 1) * side]
            lines[t, s] = part[:side].astype(jnp.bfloat16)
            lines[t, 2 * n] = cap_buf[t, n]
    turned = jnp.dot(
        backward,
        jnp.concatenate([lines[e // 4, e % 4] for e in range(edges)], axis=1),
        preferred_element_type=jnp.float32,
    ).astype(jnp.bfloat16)
    for e in range(edges):
        rims_ref[e] = jnp.where(
            flip_ref[e // 4, e % 4] == 1,
            turned[:, e * channels : (e + 1) * channels],
            lines[e // 4, e % 4],
        )
    for k in range(2 * CROSS):
        send_buf[k] = rims_ref[going[k]]

    sends = [
        pltpu.make_async_remote_copy(
            src_ref=send_buf.at[pl.ds(side_id * CROSS, CROSS)],
            dst_ref=recv_ref.at[pl.ds(side_id * CROSS, CROSS)],
            send_sem=send_sem.at[side_id],
            recv_sem=recv_sem.at[side_id],
            device_id=at(target),
            device_id_type=MESH,
        )
        for side_id, target in ((0, right), (1, left))
    ]

    def send():
        pl.semaphore_wait(barrier, 2)
        for copy in sends:
            copy.start()

    @pl.when(me == devices - 1)
    def _():
        send()

    inner_rows = side - 2

    def rows_of(chunk):
        found = []
        for k in range(ROWS):
            q = chunk * ROWS + k
            tile = tile_of(q, inner_rows, tiles)
            found.append((tile, q - inner_rows * tile + 1))
        return found

    def do_conv(chunk, parity):
        conv_rows(
            dw_ref, dw_bias_ref, cells_buf, shift_ref.at[parity], rows_of(chunk), bufs[parity]
        )

    def put(tile, row):
        def store(new):
            mid_ref[tile, row] = new[OFF : side - OFF].astype(jnp.bfloat16)
            strip_ref[tile, row, 0:OFF, :] = new[:OFF]
            strip_ref[tile, row, OFF:, :] = new[side - OFF :]

        return store

    def do_mlp(chunk, parity):
        lines = [
            (lambda a, b, tile=tile, row=row: whole_line(cells_buf, tile, row), put(tile, row))
            for tile, row in rows_of(chunk)
        ]
        mlp(w_aug_ref, w_fin_ref, bias_ref, side, lines, bufs[parity])

    chunks = tiles * inner_rows // ROWS
    bufs = (buf_a, buf_b)
    rounds = (chunks - 1) // UNROLL
    at_once = tiles if rounds < 2 or ROWS * (UNROLL + 1) > inner_rows else 1
    for copy in loads[:at_once]:
        copy.wait()
    do_conv(0, 0)
    turn = jnp.where((me == 0) | (me == devices - 1), rounds, min(1, rounds - 1))

    @pl.loop(0, rounds)
    def _(i):
        if at_once < tiles:

            @pl.when(i == 1)
            def _():
                for copy in loads[at_once:]:
                    copy.wait()

        @pl.when(i == turn)
        def _():
            send()

        for u in range(UNROLL):
            do_mlp(UNROLL * i + u, u % 2)
            do_conv(UNROLL * i + u + 1, (u + 1) % 2)

    @pl.when(me == 0)
    def _():
        send()

    for t in range(tiles):
        for s, rows in ((0, (0, 1)), (2, (side - 1, side - 2))):
            for k, row in enumerate(rows):
                line_ref[t, s, k + 1, pl.ds(OFF, side), :] = cells_buf[t, row].astype(jnp.float32)
    for c in range((chunks - 1) // UNROLL * UNROLL, chunks):
        do_mlp(c, c % 2)
        if c + 1 < chunks:
            do_conv(c + 1, (c + 1) % 2)
    for copy in sends:
        copy.wait()

    for t in range(tiles):
        lines = []
        for crosses, slot, own_edge in halo_source[4 * t : 4 * t + 4]:
            line = jnp.where(crosses, recv_ref[slot], rims_ref[own_edge])
            lines.append(line.astype(jnp.float32))
        for s, line in enumerate(lines):
            line_ref[t, s, 0, pl.ds(OFF, side), :] = line
        for s in (0, 2):
            for n, line in enumerate((lines[3], lines[1])):
                end = pl.ds(OFF + side if n else OFF - 1, 1)
                near = side - 1 if n else 0
                first = side - 1 if s else 0
                second = side - 2 if s else 1
                line_ref[t, s, 0, end, :] = 0.5 * (
                    lines[s][near : near + 1] + line[first : first + 1]
                )
                line_ref[t, s, 1, end, :] = line[first : first + 1]
                line_ref[t, s, 2, end, :] = line[second : second + 1]


def edge_kernel(
    mid_ref,
    strip_in_ref,
    line_ref,
    w_aug_ref,
    w_fin_ref,
    dw_ref,
    dw_bias_ref,
    bias_ref,
    out_hbm,
    strip_ref,
    caps_ref,
    sides_ref,
    buf_a,
    buf_b,
    mid_sem,
    cap_sem,
    side_sem,
):
    tiles, side, _, channels = out_hbm.shape
    mid_copies = [
        pltpu.make_async_copy(
            mid_ref.at[t, pl.ds(1, side - 2)],
            out_hbm.at[t, pl.ds(1, side - 2), pl.ds(OFF, side - 2 * OFF)],
            mid_sem.at[t],
        )
        for t in range(tiles)
    ]
    for copy in mid_copies:
        copy.start()
    fill_ones(buf_a)
    fill_ones(buf_b)
    flat_strip = strip_ref.reshape(tiles * side * 2 * OFF, channels)

    def put_cap(tile, n):
        def store(new):
            caps_ref[tile, n] = new.astype(jnp.bfloat16)

        return store

    def put_side(tile, n):
        first = tile * side * 2 * OFF + n * (2 * OFF - 1)

        def store(new):
            flat_strip[pl.ds(first, side, stride=2 * OFF), :] = new

        return store

    def lines_of(tile):
        return [
            (rim_lines(line_ref, side, tile, s), store)
            for s, store in (
                (0, put_cap(tile, 0)),
                (2, put_cap(tile, 1)),
                (3, put_side(tile, 0)),
                (1, put_side(tile, 1)),
            )
        ]

    groups = [
        [line for t in range(g, g + 2) for line in lines_of(t)] for g in range(0, tiles, 2)
    ]
    bufs = (buf_a, buf_b)
    copies = []

    def finish(g):
        for t in (2 * g, 2 * g + 1):
            for n, row in enumerate((0, side - 1)):
                copies.append(
                    pltpu.make_async_copy(
                        caps_ref.at[t, n], out_hbm.at[t, row], cap_sem.at[t, n]
                    )
                )
                copies[-1].start()
            for n, col in enumerate((0, side - OFF)):
                sides_ref[t, n] = strip_ref[t, :, n * OFF : (n + 1) * OFF, :].astype(jnp.bfloat16)
                copies.append(
                    pltpu.make_async_copy(
                        sides_ref.at[t, n, pl.ds(1, side - 2)],
                        out_hbm.at[t, pl.ds(1, side - 2), pl.ds(col, OFF)],
                        side_sem.at[t, n],
                    )
                )
                copies[-1].start()

    for g, group in enumerate(groups):
        conv(dw_ref, dw_bias_ref, side, [load for load, _ in group], bufs[g % 2])
        if g:
            mlp(w_aug_ref, w_fin_ref, bias_ref, side, groups[g - 1], bufs[(g - 1) % 2])
            finish(g - 1)
    mlp(w_aug_ref, w_fin_ref, bias_ref, side, groups[-1], bufs[(len(groups) - 1) % 2])
    finish(len(groups) - 1)
    for copy in mid_copies + copies:
        copy.wait()


def per_device(sizes, cells, *rest):
    tables, (dw_weight, dw_bias, ln_gain, ln_bias, w_in, b_in, w_out, b_out, layer_scale) = (
        rest[:2],
        rest[2:],
    )
    tiles, side, _, channels = cells.shape
    hidden = w_in.shape[0]
    edges = 4 * tiles
    vmem = pl.BlockSpec(memory_space=pltpu.VMEM)
    anywhere = pl.BlockSpec(memory_space=pltpu.HBM)
    dw_bias, ln_gain, ln_bias, b_out, layer_scale = (
        vector.reshape(1, channels)
        for vector in (dw_bias, ln_gain, ln_bias, b_out, layer_scale)
    )
    operands = [
        pltpu.with_memory_space_constraint(array, pltpu.HBM)
        for array in (
            cells,
            *tables,
            dw_weight,
            dw_bias,
            ln_gain,
            ln_bias,
            w_in,
            b_in,
            w_out,
            b_out,
            layer_scale,
        )
    ]
    strip_shape = (tiles, side, 2 * OFF, channels)
    vector = pltpu.VMEM((1, channels), jnp.float32)
    buffers = [pltpu.VMEM((ROWS * side, 2 * channels), jnp.bfloat16)] * 2
    passed = pl.pallas_call(
        functools.partial(inner_kernel, sizes),
        out_shape=(
            pltpu.VMEM((tiles, side, side - 2 * OFF, channels), jnp.bfloat16),
            pltpu.VMEM(strip_shape, jnp.float32),
            pltpu.VMEM((tiles, 4, 3, side + 2 * OFF, channels), jnp.float32),
            pltpu.VMEM((2 * channels, hidden), jnp.bfloat16),
            pltpu.VMEM((hidden, channels), jnp.bfloat16),
            pltpu.VMEM(dw_weight.shape, jnp.float32),
            vector,
            vector,
        ),
        in_specs=[anywhere] * len(operands),
        out_specs=(vmem,) * 8,
        scratch_shapes=[
            pltpu.VMEM(cells.shape, jnp.bfloat16),
            pltpu.VMEM((tiles, 2, side, OFF, channels), jnp.bfloat16),
            pltpu.VMEM((tiles, 2, side, channels), jnp.bfloat16),
            pltpu.VMEM((edges, side, channels), jnp.bfloat16),
            pltpu.VMEM((2 * CROSS, side, channels), jnp.bfloat16),
            pltpu.VMEM((2 * CROSS, side, channels), jnp.bfloat16),
            *buffers,
            pltpu.VMEM((2, ROWS, 2, side + 2 * OFF, channels), jnp.float32),
            pltpu.SMEM(tables[0].shape, jnp.int32),
            pltpu.SMEM(tables[1].shape, jnp.int32),
            vector,
            vector,
            pltpu.VMEM(w_in.shape, jnp.bfloat16),
            pltpu.VMEM(b_in.shape, jnp.bfloat16),
            pltpu.VMEM(w_out.shape, jnp.bfloat16),
            vector,
            vector,
            pltpu.SemaphoreType.DMA((tiles,)),
            pltpu.SemaphoreType.DMA((tiles, 2)),
            pltpu.SemaphoreType.DMA((tiles, 2)),
            pltpu.SemaphoreType.DMA((2,)),
            pltpu.SemaphoreType.DMA((9,)),
            pltpu.SemaphoreType.DMA((2,)),
            pltpu.SemaphoreType.DMA((2,)),
        ],
        compiler_params=pltpu.CompilerParams(
            collective_id=0, has_side_effects=True, vmem_limit_bytes=GRANT
        ),
        name="inner",
    )(*operands)
    return pl.pallas_call(
        edge_kernel,
        out_shape=(
            jax.ShapeDtypeStruct(cells.shape, jnp.bfloat16),
            pltpu.VMEM(strip_shape, jnp.float32),
        ),
        in_specs=[vmem] * 8,
        out_specs=(anywhere, vmem),
        input_output_aliases={1: 1},
        scratch_shapes=[
            pltpu.VMEM((tiles, 2, side, channels), jnp.bfloat16),
            pltpu.VMEM((tiles, 2, side, OFF, channels), jnp.bfloat16),
            *buffers,
            pltpu.SemaphoreType.DMA((tiles,)),
            pltpu.SemaphoreType.DMA((tiles, 2)),
            pltpu.SemaphoreType.DMA((tiles, 2)),
        ],
        compiler_params=pltpu.CompilerParams(vmem_limit_bytes=GRANT),
        name="edge",
    )(*passed)[0]


def solution(mesh):
    spread_spec = P(AXES, None, None, None)
    in_specs = (spread_spec, P(AXES, None), P(AXES, None)) + (P(),) * 9
    sizes = (mesh.shape["tile"], mesh.shape["hidden"])
    return jax.shard_map(
        functools.partial(per_device, sizes),
        mesh=mesh,
        in_specs=in_specs,
        out_specs=spread_spec,
        check_vma=False,
    )
```

```python
import functools

import jax
import jax.numpy as jnp
from jax import lax
from jax.experimental import pallas as pl
from jax.experimental.pallas import tpu as pltpu
from jax.sharding import PartitionSpec as P

AXES = ("tile", "hidden")
OFF = 8
ROWS = 8
UNROLL = 8
CROSS = 4
GRANT = 40 * 1024 * 1024
MESH = pl.DeviceIdType.MESH
ROOT_HALF = 0.7071067811865476


def tile_of(q, per_tile, tiles):
    tile = 0
    for j in range(1, tiles):
        tile = tile + jnp.where(q >= j * per_tile, 1, 0)
    return tile


def rim_lines(line_ref, length, tile, s):
    def load(a, b):
        across, along = (a, b) if s % 2 == 0 else (b, a)
        return line_ref[tile, s, across if s in (0, 3) else 2 - across, pl.ds(OFF - 1 + along, length), :]

    return load


def normed(total, eps):
    center = total - jnp.mean(total, axis=-1, keepdims=True)
    spread = jnp.sum(center * center, axis=-1, keepdims=True)
    return (center * lax.rsqrt(spread + eps)).astype(jnp.bfloat16)


def conv(dw_ref, dw_bias_ref, side, segments, dst):
    channels = dw_ref.shape[1]
    for n, load in enumerate(segments):
        total = jnp.broadcast_to(dw_bias_ref[...], (side, channels))
        for a in range(3):
            for b in range(3):
                total = total + dw_ref[3 * a + b : 3 * a + b + 1] * load(a, b)
        dst[n * side : (n + 1) * side, 0:channels] = normed(total, 1e-06 * channels)


def whole_line(cells_buf, tile, row):
    side, step = cells_buf.shape[2], 2 * OFF
    return jnp.concatenate(
        [cells_buf[tile, row, n : n + step] for n in range(0, side, step)], axis=0
    )


def conv_rows(dw_ref, dw_bias_ref, cells_buf, shift_ref, rows, dst):
    side, channels = cells_buf.shape[2:]
    taps = [
        jnp.broadcast_to(dw_ref[k : k + 1], (side, channels)).astype(jnp.bfloat16)
        for k in range(9)
    ]
    for n, (tile, row) in enumerate(rows):
        lines = [
            whole_line(cells_buf, tile, row - 1 + a) for a in range(3)
        ]
        sums = []
        for b in range(3):
            part = taps[b] * lines[0]
            for a in range(1, 3):
                part = part + taps[3 * a + b] * lines[a]
            sums.append(part.astype(jnp.float32))
        shift_ref[n, 0, pl.ds(OFF, side), :] = sums[0]
        shift_ref[n, 1, pl.ds(OFF, side), :] = sums[2]
        total = (sums[1] + dw_bias_ref[...]) + (
            shift_ref[n, 0, pl.ds(OFF - 1, side), :] + shift_ref[n, 1, pl.ds(OFF + 1, side), :]
        )
        dst[n * side : (n + 1) * side, 0:channels] = normed(total, 1e-06 * channels)


def mlp(w_aug_ref, w_fin_ref, bias_ref, side, segments, src):
    z = jnp.dot(src[...], w_aug_ref[...], preferred_element_type=jnp.float32)
    z = z.astype(jnp.bfloat16)
    act = z * (lax.erf(z) + jnp.bfloat16(1))
    mixed = jnp.dot(act, w_fin_ref[...], preferred_element_type=jnp.float32)
    for n, (load, store) in enumerate(segments):
        store(load(1, 1).astype(jnp.float32) + (mixed[n * side : (n + 1) * side] + bias_ref[...]))


def fill_ones(buf):
    rows, both = buf.shape
    lane = lax.broadcasted_iota(jnp.int32, (rows, both // 2), 1)
    buf[:, both // 2 :] = jnp.where(lane < 2, 1.0, 0.0).astype(jnp.bfloat16)


def last_flagged(flags, values):
    found = [jnp.int32(0)] * CROSS
    for flag, value in zip(flags, values):
        for k in range(CROSS - 1, 0, -1):
            found[k] = jnp.where(flag, found[k - 1], found[k])
        found[0] = jnp.where(flag, value, found[0])
    return found


def owned(partner, device, edges):
    local = partner - device * edges
    return (local >= 0) & (local < edges), local


def above(values, limit):
    return sum(jnp.where(value > limit, 1, 0) for value in values)


def split_bf16(value):
    high = value.astype(jnp.bfloat16).astype(jnp.float32)
    return high, value - high


def fold_weights(gain_ref, ln_bias_ref, w_in, b_in, w_out, b_out_ref, scale_ref, w_aug_ref, w_fin_ref, bias_ref):
    hidden, channels = w_in.shape
    eye = (
        lax.broadcasted_iota(jnp.int32, (channels, channels), 0)
        == lax.broadcasted_iota(jnp.int32, (channels, channels), 1)
    ).astype(jnp.bfloat16)
    gain = gain_ref[...] * (ROOT_HALF * channels**0.5)
    w_gain = (w_in.astype(jnp.float32) * gain).astype(jnp.bfloat16)
    turned = (((1,), (1,)), ((), ()))
    w_aug_ref[0:channels, :] = lax.dot_general(
        eye, w_gain, turned, preferred_element_type=jnp.float32
    ).astype(jnp.bfloat16)
    high, rest = split_bf16(ln_bias_ref[...])
    middle, low = split_bf16(rest)
    row_id = lax.broadcasted_iota(jnp.int32, (16, channels), 0)
    parts = jnp.where(
        row_id == 0, high, jnp.where(row_id == 1, middle, jnp.where(row_id == 2, low, 0.0))
    ).astype(jnp.bfloat16)
    moved = lax.dot_general(parts, w_in, turned, preferred_element_type=jnp.float32)
    moved = jnp.sum(moved, axis=0, keepdims=True)
    total = (b_in.astype(jnp.float32).reshape(1, hidden) + moved) * ROOT_HALF
    high, rest = split_bf16(total)
    row_id = lax.broadcasted_iota(jnp.int32, (channels, hidden), 0)
    extra = jnp.where(row_id == 0, high, jnp.where(row_id == 1, rest, 0.0))
    w_aug_ref[channels : 2 * channels, :] = extra.astype(jnp.bfloat16)
    scale = scale_ref[...]
    w_fin_ref[...] = (w_out.astype(jnp.float32) * (scale * ROOT_HALF)).astype(jnp.bfloat16)
    bias_ref[...] = scale * b_out_ref[...]


def inner_kernel(
    sizes,
    cells_ref,
    partner_hbm,
    flip_hbm,
    dw_hbm,
    dw_bias_hbm,
    gain_hbm,
    ln_bias_hbm,
    w_in_hbm,
    b_in_hbm,
    w_out_hbm,
    b_out_hbm,
    scale_hbm,
    mid_ref,
    strip_ref,
    line_ref,
    w_aug_ref,
    w_fin_ref,
    dw_ref,
    dw_bias_ref,
    bias_ref,
    cells_buf,
    side_buf,
    cap_buf,
    rims_ref,
    recv_ref,
    send_buf,
    buf_a,
    buf_b,
    shift_ref,
    partner_ref,
    flip_ref,
    gain_ref,
    ln_bias_ref,
    w_in_ref,
    b_in_ref,
    w_out_ref,
    b_out_ref,
    scale_ref,
    load_sem,
    cap_sem,
    side_sem,
    table_sem,
    weight_sem,
    send_sem,
    recv_sem,
):
    tile_devices, hidden_devices = sizes
    tiles, side, _, channels = cells_ref.shape
    edges = 4 * tiles
    devices = tile_devices * hidden_devices
    me = lax.axis_index("tile") * hidden_devices + lax.axis_index("hidden")

    def at(position):
        return (position // hidden_devices, position % hidden_devices)

    right = lax.rem(me + 1, devices)
    left = lax.rem(me + devices - 1, devices)
    tables = [
        pltpu.make_async_copy(src, dst, table_sem.at[n])
        for n, (src, dst) in enumerate(((partner_hbm, partner_ref), (flip_hbm, flip_ref)))
    ]
    caps = [
        pltpu.make_async_copy(cells_ref.at[t, row], cap_buf.at[t, n], cap_sem.at[t, n])
        for t in range(tiles)
        for n, row in enumerate((0, side - 1))
    ]
    borders = [
        pltpu.make_async_copy(
            cells_ref.at[t, :, pl.ds(col, OFF)], side_buf.at[t, n], side_sem.at[t, n]
        )
        for t in range(tiles)
        for n, col in enumerate((0, side - OFF))
    ]
    loads = [
        pltpu.make_async_copy(cells_ref.at[t], cells_buf.at[t], load_sem.at[t])
        for t in range(tiles)
    ]
    weights = [
        pltpu.make_async_copy(src, dst, weight_sem.at[n])
        for n, (src, dst) in enumerate(
            (
                (w_in_hbm, w_in_ref),
                (w_out_hbm, w_out_ref),
                (b_in_hbm, b_in_ref),
                (gain_hbm, gain_ref),
                (ln_bias_hbm, ln_bias_ref),
                (b_out_hbm, b_out_ref),
                (scale_hbm, scale_ref),
                (dw_hbm, dw_ref),
                (dw_bias_hbm, dw_bias_ref),
            )
        )
    ]
    for copy in tables + weights + caps + borders + loads:
        copy.start()
    barrier = pltpu.get_barrier_semaphore()
    for neighbour in (left, right):
        pl.semaphore_signal(barrier, inc=1, device_id=at(neighbour), device_id_type=MESH)

    fill_ones(buf_a)
    fill_ones(buf_b)
    for copy in tables:
        copy.wait()
    for copy in weights:
        copy.wait()
    fold_weights(
        gain_ref,
        ln_bias_ref,
        w_in_ref[...],
        b_in_ref[...],
        w_out_ref[...],
        b_out_ref,
        scale_ref,
        w_aug_ref,
        w_fin_ref,
        bias_ref,
    )

    def one_hot(found):
        return jnp.where(found, 1.0, 0.0).astype(jnp.bfloat16)

    r_id = lax.broadcasted_iota(jnp.int32, (side, side), 0)
    c_id = lax.broadcasted_iota(jnp.int32, (side, side), 1)
    backward = one_hot(c_id + r_id == side - 1)
    r_id = lax.broadcasted_iota(jnp.int32, (side, side * OFF), 0)
    c_id = lax.broadcasted_iota(jnp.int32, (side, side * OFF), 1)
    picks = [
        jnp.concatenate(
            [one_hot(c_id - OFF * r_id == (OFF - 1 - k if n else k)) for k in range(2)], axis=0
        )
        for n in range(2)
    ]
    for copy in caps + borders:
        copy.wait()
    partners = [partner_ref[e // 4, e % 4] for e in range(edges)]
    local = [jnp.int32(e) for e in range(edges)]
    going = []
    for device in (right, left):
        going += last_flagged([owned(p, device, edges)[0] for p in partners], local)

    prev_flags, prev_local = zip(*[owned(p, left, edges) for p in partners])
    next_flags, next_local = zip(*[owned(p, right, edges) for p in partners])
    prev_list = last_flagged(prev_flags, prev_local)
    next_list = last_flagged(next_flags, next_local)
    halo_source = []
    for e in range(edges):
        slot = jnp.where(
            prev_flags[e],
            above(prev_list, prev_local[e]),
            CROSS + above(next_list, next_local[e]),
        )
        crosses = prev_flags[e] | next_flags[e]
        own_edge = jnp.clip(jnp.where(crosses, 0, partners[e] - me * edges), 0, edges - 1)
        slot = jnp.clip(jnp.where(crosses, slot, 0), 0, 2 * CROSS - 1)
        halo_source.append((crosses, slot, own_edge))

    lines = {}
    for n, s in enumerate((3, 1)):
        both = jnp.dot(
            picks[n],
            jnp.concatenate(
                [side_buf[t, n].reshape(side * OFF, channels) for t in range(tiles)], axis=1
            ),
            preferred_element_type=jnp.float32,
        )
        for t in range(tiles):
            part = both[:, t * channels : (t + 1) * channels]
            for k in range(2):
                line_ref[t, s, k + 1, pl.ds(OFF, side), :] = part[k * side : (k + 1) * side]
            lines[t, s] = part[:side].astype(jnp.bfloat16)
            lines[t, 2 * n] = cap_buf[t, n]
    turned = jnp.dot(
        backward,
        jnp.concatenate([lines[e // 4, e % 4] for e in range(edges)], axis=1),
        preferred_element_type=jnp.float32,
    ).astype(jnp.bfloat16)
    for e in range(edges):
        rims_ref[e] = jnp.where(
            flip_ref[e // 4, e % 4] == 1,
            turned[:, e * channels : (e + 1) * channels],
            lines[e // 4, e % 4],
        )
    for k in range(2 * CROSS):
        send_buf[k] = rims_ref[going[k]]

    sends = [
        pltpu.make_async_remote_copy(
            src_ref=send_buf.at[pl.ds(side_id * CROSS, CROSS)],
            dst_ref=recv_ref.at[pl.ds(side_id * CROSS, CROSS)],
            send_sem=send_sem.at[side_id],
            recv_sem=recv_sem.at[side_id],
            device_id=at(target),
            device_id_type=MESH,
        )
        for side_id, target in ((0, right), (1, left))
    ]

    def send():
        pl.semaphore_wait(barrier, 2)
        for copy in sends:
            copy.start()

    @pl.when(me == devices - 1)
    def _():
        send()

    inner_rows = side - 2

    def rows_of(chunk):
        found = []
        for k in range(ROWS):
            q = chunk * ROWS + k
            tile = tile_of(q, inner_rows, tiles)
            found.append((tile, q - inner_rows * tile + 1))
        return found

    def do_conv(chunk, parity):
        conv_rows(
            dw_ref, dw_bias_ref, cells_buf, shift_ref.at[parity], rows_of(chunk), bufs[parity]
        )

    def put(tile, row):
        def store(new):
            mid_ref[tile, row] = new[OFF : side - OFF].astype(jnp.bfloat16)
            strip_ref[tile, row, 0:OFF, :] = new[:OFF]
            strip_ref[tile, row, OFF:, :] = new[side - OFF :]

        return store

    def do_mlp(chunk, parity):
        lines = [
            (lambda a, b, tile=tile, row=row: whole_line(cells_buf, tile, row), put(tile, row))
            for tile, row in rows_of(chunk)
        ]
        mlp(w_aug_ref, w_fin_ref, bias_ref, side, lines, bufs[parity])

    chunks = tiles * inner_rows // ROWS
    bufs = (buf_a, buf_b)
    rounds = (chunks - 1) // UNROLL
    at_once = tiles if rounds < 2 or ROWS * (UNROLL + 1) > inner_rows else 1
    for copy in loads[:at_once]:
        copy.wait()
    do_conv(0, 0)
    turn = jnp.where((me == 0) | (me == devices - 1), rounds, min(1, rounds - 1))

    @pl.loop(0, rounds)
    def _(i):
        if at_once < tiles:

            @pl.when(i == 1)
            def _():
                for copy in loads[at_once:]:
                    copy.wait()

        @pl.when(i == turn)
        def _():
            send()

        for u in range(UNROLL):
            do_mlp(UNROLL * i + u, u % 2)
            do_conv(UNROLL * i + u + 1, (u + 1) % 2)

    @pl.when(me == 0)
    def _():
        send()

    for t in range(tiles):
        for s, rows in ((0, (0, 1)), (2, (side - 1, side - 2))):
            for k, row in enumerate(rows):
                line_ref[t, s, k + 1, pl.ds(OFF, side), :] = cells_buf[t, row].astype(jnp.float32)
    for c in range((chunks - 1) // UNROLL * UNROLL, chunks):
        do_mlp(c, c % 2)
        if c + 1 < chunks:
            do_conv(c + 1, (c + 1) % 2)
    for copy in sends:
        copy.wait()

    for t in range(tiles):
        lines = []
        for crosses, slot, own_edge in halo_source[4 * t : 4 * t + 4]:
            line = jnp.where(crosses, recv_ref[slot], rims_ref[own_edge])
            lines.append(line.astype(jnp.float32))
        for s, line in enumerate(lines):
            line_ref[t, s, 0, pl.ds(OFF, side), :] = line
        for s in (0, 2):
            for n, line in enumerate((lines[3], lines[1])):
                end = pl.ds(OFF + side if n else OFF - 1, 1)
                near = side - 1 if n else 0
                first = side - 1 if s else 0
                second = side - 2 if s else 1
                line_ref[t, s, 0, end, :] = 0.5 * (
                    lines[s][near : near + 1] + line[first : first + 1]
                )
                line_ref[t, s, 1, end, :] = line[first : first + 1]
                line_ref[t, s, 2, end, :] = line[second : second + 1]


def edge_kernel(
    mid_ref,
    strip_in_ref,
    line_ref,
    w_aug_ref,
    w_fin_ref,
    dw_ref,
    dw_bias_ref,
    bias_ref,
    out_hbm,
    strip_ref,
    caps_ref,
    sides_ref,
    buf_a,
    buf_b,
    mid_sem,
    cap_sem,
    side_sem,
):
    tiles, side, _, channels = out_hbm.shape
    mid_copies = [
        pltpu.make_async_copy(
            mid_ref.at[t, pl.ds(1, side - 2)],
            out_hbm.at[t, pl.ds(1, side - 2), pl.ds(OFF, side - 2 * OFF)],
            mid_sem.at[t],
        )
        for t in range(tiles)
    ]
    for copy in mid_copies:
        copy.start()
    fill_ones(buf_a)
    fill_ones(buf_b)
    flat_strip = strip_ref.reshape(tiles * side * 2 * OFF, channels)

    def put_cap(tile, n):
        def store(new):
            caps_ref[tile, n] = new.astype(jnp.bfloat16)

        return store

    def put_side(tile, n):
        first = tile * side * 2 * OFF + n * (2 * OFF - 1)

        def store(new):
            flat_strip[pl.ds(first, side, stride=2 * OFF), :] = new

        return store

    def lines_of(tile):
        return [
            (rim_lines(line_ref, side, tile, s), store)
            for s, store in (
                (0, put_cap(tile, 0)),
                (2, put_cap(tile, 1)),
                (3, put_side(tile, 0)),
                (1, put_side(tile, 1)),
            )
        ]

    groups = [
        [line for t in range(g, g + 2) for line in lines_of(t)] for g in range(0, tiles, 2)
    ]
    bufs = (buf_a, buf_b)
    copies = []

    def finish(g):
        for t in (2 * g, 2 * g + 1):
            for n, row in enumerate((0, side - 1)):
                copies.append(
                    pltpu.make_async_copy(
                        caps_ref.at[t, n], out_hbm.at[t, row], cap_sem.at[t, n]
                    )
                )
                copies[-1].start()
            for n, col in enumerate((0, side - OFF)):
                sides_ref[t, n] = strip_ref[t, :, n * OFF : (n + 1) * OFF, :].astype(jnp.bfloat16)
                copies.append(
                    pltpu.make_async_copy(
                        sides_ref.at[t, n, pl.ds(1, side - 2)],
                        out_hbm.at[t, pl.ds(1, side - 2), pl.ds(col, OFF)],
                        side_sem.at[t, n],
                    )
                )
                copies[-1].start()

    for g, group in enumerate(groups):
        conv(dw_ref, dw_bias_ref, side, [load for load, _ in group], bufs[g % 2])
        if g:
            mlp(w_aug_ref, w_fin_ref, bias_ref, side, groups[g - 1], bufs[(g - 1) % 2])
            finish(g - 1)
    mlp(w_aug_ref, w_fin_ref, bias_ref, side, groups[-1], bufs[(len(groups) - 1) % 2])
    finish(len(groups) - 1)
    for copy in mid_copies + copies:
        copy.wait()


def per_device(sizes, cells, *rest):
    tables, (dw_weight, dw_bias, ln_gain, ln_bias, w_in, b_in, w_out, b_out, layer_scale) = (
        rest[:2],
        rest[2:],
    )
    tiles, side, _, channels = cells.shape
    hidden = w_in.shape[0]
    edges = 4 * tiles
    vmem = pl.BlockSpec(memory_space=pltpu.VMEM)
    anywhere = pl.BlockSpec(memory_space=pltpu.HBM)
    dw_bias, ln_gain, ln_bias, b_out, layer_scale = (
        vector.reshape(1, channels)
        for vector in (dw_bias, ln_gain, ln_bias, b_out, layer_scale)
    )
    operands = [
        pltpu.with_memory_space_constraint(array, pltpu.HBM)
        for array in (
            cells,
            *tables,
            dw_weight,
            dw_bias,
            ln_gain,
            ln_bias,
            w_in,
            b_in,
            w_out,
            b_out,
            layer_scale,
        )
    ]
    strip_shape = (tiles, side, 2 * OFF, channels)
    vector = pltpu.VMEM((1, channels), jnp.float32)
    buffers = [pltpu.VMEM((ROWS * side, 2 * channels), jnp.bfloat16)] * 2
    passed = pl.pallas_call(
        functools.partial(inner_kernel, sizes),
        out_shape=(
            pltpu.VMEM((tiles, side, side - 2 * OFF, channels), jnp.bfloat16),
            pltpu.VMEM(strip_shape, jnp.float32),
            pltpu.VMEM((tiles, 4, 3, side + 2 * OFF, channels), jnp.float32),
            pltpu.VMEM((2 * channels, hidden), jnp.bfloat16),
            pltpu.VMEM((hidden, channels), jnp.bfloat16),
            pltpu.VMEM(dw_weight.shape, jnp.float32),
            vector,
            vector,
        ),
        in_specs=[anywhere] * len(operands),
        out_specs=(vmem,) * 8,
        scratch_shapes=[
            pltpu.VMEM(cells.shape, jnp.bfloat16),
            pltpu.VMEM((tiles, 2, side, OFF, channels), jnp.bfloat16),
            pltpu.VMEM((tiles, 2, side, channels), jnp.bfloat16),
            pltpu.VMEM((edges, side, channels), jnp.bfloat16),
            pltpu.VMEM((2 * CROSS, side, channels), jnp.bfloat16),
            pltpu.VMEM((2 * CROSS, side, channels), jnp.bfloat16),
            *buffers,
            pltpu.VMEM((2, ROWS, 2, side + 2 * OFF, channels), jnp.float32),
            pltpu.SMEM(tables[0].shape, jnp.int32),
            pltpu.SMEM(tables[1].shape, jnp.int32),
            vector,
            vector,
            pltpu.VMEM(w_in.shape, jnp.bfloat16),
            pltpu.VMEM(b_in.shape, jnp.bfloat16),
            pltpu.VMEM(w_out.shape, jnp.bfloat16),
            vector,
            vector,
            pltpu.SemaphoreType.DMA((tiles,)),
            pltpu.SemaphoreType.DMA((tiles, 2)),
            pltpu.SemaphoreType.DMA((tiles, 2)),
            pltpu.SemaphoreType.DMA((2,)),
            pltpu.SemaphoreType.DMA((9,)),
            pltpu.SemaphoreType.DMA((2,)),
            pltpu.SemaphoreType.DMA((2,)),
        ],
        compiler_params=pltpu.CompilerParams(
            collective_id=0, has_side_effects=True, vmem_limit_bytes=GRANT
        ),
        name="inner",
    )(*operands)
    return pl.pallas_call(
        edge_kernel,
        out_shape=(
            jax.ShapeDtypeStruct(cells.shape, jnp.bfloat16),
            pltpu.VMEM(strip_shape, jnp.float32),
        ),
        in_specs=[vmem] * 8,
        out_specs=(anywhere, vmem),
        input_output_aliases={1: 1},
        scratch_shapes=[
            pltpu.VMEM((tiles, 2, side, channels), jnp.bfloat16),
            pltpu.VMEM((tiles, 2, side, OFF, channels), jnp.bfloat16),
            *buffers,
            pltpu.SemaphoreType.DMA((tiles,)),
            pltpu.SemaphoreType.DMA((tiles, 2)),
            pltpu.SemaphoreType.DMA((tiles, 2)),
        ],
        compiler_params=pltpu.CompilerParams(vmem_limit_bytes=GRANT),
        name="edge",
    )(*passed)[0]


def solution(mesh):
    spread_spec = P(AXES, None, None, None)
    in_specs = (spread_spec, P(AXES, None), P(AXES, None)) + (P(),) * 9
    sizes = (mesh.shape["tile"], mesh.shape["hidden"])
    return jax.shard_map(
        functools.partial(per_device, sizes),
        mesh=mesh,
        in_specs=in_specs,
        out_specs=spread_spec,
        check_vma=False,
    )
```
